32 devices in a mesh: grp: 2 (over y), gz: 4 (over z), af: 4 (over x, core).
Axes of the slice: x: 2, y: 2, z: 4, core: 2. Of those that a mesh axis runs over, the one named last changes fastest.
Arguments:
- volume: float32 [64, 16, 16, 256], P('af', ('grp', 'gz')), parts along dimension 1, may hold values from -6 to 6
- out_grad: float32 [128, 8, 8, 128], P('af', ('grp', 'gz')), parts along dimension 1, may hold values from -6 to 6
- weight: float32 [128, 1728], P('af'), may hold values from -0.15625 to 0.15625
Outputs:
- input_grad: float32 [64, 16, 16, 256], P('af', ('grp', 'gz')), parts along dimension 1
- weight_grad: float32 [128, 3456], P('af', 'grp'), parts along dimension 1
The draws below stay inside these ranges and needn't reach their ends.
There are 2 independent parts, one for each index of `grp`. The reference program is written for one: setup_inputs(seed, part) draws one part's arguments, and reference() takes and returns one part's arrays. A program takes and returns all parts, laid end to end along the dimension named above; an argument that names none is the same for every part. Nothing has to cross between parts.
All inputs are finite; a program needn't handle non-finite values.
Results may differ from the reference program's by a relative error of at most 0.0003.
Values sent between devices are 32-bit elements; how exact they have to be, the bound alone decides.
No kernel may reach another device: no remote copies, remote signals or barrier semaphores. Data moves between devices by JAX's collectives and lax.ppermute only.
A program may use at most 128 MiB of HBM per device.

```python
import math
import jax
import jax.numpy as jnp
from jax import lax

CIN = 64
COUT = 128
Y = 16
X = 256
YO = 8
XO = 128
NZ = 8
NZO = 4


def shard_levels(key, dims, cuts, low, top_value):
    factor_of, own = 1.0, jax.random.fold_in(key, 6)
    for dim, blocks in cuts:
        steps = jnp.exp(jax.random.uniform(jax.random.fold_in(own, dim), (blocks,), jnp.float32, low / len(cuts), top_value / len(cuts)))
        factor_of = factor_of * jnp.repeat(steps, dims[dim] // blocks).reshape([-1 if axis == dim else 1 for axis in range(len(dims))])
    return factor_of


def scatter_about(stream_key, extent, deviation, reach, shards=(), kind=jnp.bfloat16):
    array = jax.random.normal(stream_key, extent, jnp.float32) * deviation
    if len(shards) > 0:
        array = shard_levels(stream_key, extent, shards, -0.22, 0.18) * array
    return jnp.clip(array, min=-reach, max=reach).astype(kind)


def setup_inputs(seed: int = 0, part: int = 0) -> dict:
    key_of = jax.random.split(jax.random.key(seed), 4)
    part_keys = jax.random.split(jax.random.fold_in(key_of[3], part), 4)
    return {
        "volume": scatter_about(part_keys[0], (CIN, NZ, Y, X), 1.0, 6.0, ((0, 4), (1, 4)), jnp.float32),
        "out_grad": scatter_about(part_keys[1], (COUT, NZO, YO, XO), 1.0, 6.0, ((0, 4), (1, 4)), jnp.float32),
        "weight": scatter_about(key_of[2], (COUT, 27 * CIN), (27 * CIN) ** -0.5, 0.15625, ((0, 4),), jnp.float32),
    }


def tap_matrix(extended, out_depth, out_rows, out_cols):
    channels = extended.shape[0]
    padded = jnp.pad(extended, ((0, 0), (0, 1), (1, 1), (1, 1)))
    split = padded.reshape(channels, out_depth + 1, 2, out_rows + 1, 2, out_cols + 1, 2)
    pieces = []
    for depth_tap in range(3):
        for row_tap in range(3):
            for col_tap in range(3):
                dz_lo = depth_tap // 2
                dy_lo = row_tap // 2
                dx_lo = col_tap // 2
                pieces.append(split[:, dz_lo:dz_lo + out_depth, depth_tap % 2, dy_lo:dy_lo + out_rows, row_tap % 2, dx_lo:dx_lo + out_cols, col_tap % 2])
    stacked = jnp.stack(pieces, axis=0)
    return stacked.reshape(27 * channels, out_depth * out_rows * out_cols)

def place_terms(tap_terms, channels, depth_count, out_rows, out_cols, planes, rows, cols):
    shaped = tap_terms.reshape(27, channels, depth_count, out_rows, out_cols)
    phases = {}
    for depth_tap in range(3):
        for row_tap in range(3):
            for col_tap in range(3):
                index = 9 * depth_tap + 3 * row_tap + col_tap
                dz_lo = depth_tap // 2
                dy_lo = row_tap // 2
                dx_lo = col_tap // 2
                moved = jnp.pad(shaped[index], ((0, 0), (dz_lo, 1 - dz_lo), (dy_lo, 1 - dy_lo), (dx_lo, 1 - dx_lo)))
                parity = (depth_tap % 2, row_tap % 2, col_tap % 2)
                phases[parity] = moved if parity not in phases else phases[parity] + moved
    depth_pairs = []
    for depth_bit in range(2):
        row_pairs = []
        for row_bit in range(2):
            col_pair = jnp.stack([phases[depth_bit, row_bit, 0], phases[depth_bit, row_bit, 1]], axis=-1)
            row_pairs.append(col_pair)
        depth_pairs.append(jnp.stack(row_pairs, axis=3))
    woven = jnp.stack(depth_pairs, axis=2)
    canvas = woven.reshape(channels, 2 * (depth_count + 1), 2 * (out_rows + 1), 2 * (out_cols + 1))
    return canvas[:, 1:planes + 1, 1:rows + 1, 1:cols + 1]

def reference(volume, out_grad, weight):
    channels, planes, rows, cols = volume.shape
    filters, out_depth, out_rows, out_cols = out_grad.shape
    factor = 1.0 / math.sqrt(out_depth * out_rows * out_cols)
    extended = jnp.concatenate([jnp.zeros((channels, 1, rows, cols), volume.dtype), volume], axis=1)
    tap_rows = tap_matrix(extended, out_depth, out_rows, out_cols)
    weight_grad = lax.dot_general(out_grad.reshape(filters, -1), tap_rows, (((1,), (1,)), ((), ())), precision=lax.Precision.HIGHEST, preferred_element_type=jnp.float32) * factor
    grad_ext = jnp.concatenate([out_grad, jnp.zeros((filters, 1, out_rows, out_cols), out_grad.dtype)], axis=1)
    tap_terms = lax.dot_general(weight, grad_ext.reshape(filters, -1), (((0,), (0,)), ((), ())), precision=lax.Precision.HIGHEST, preferred_element_type=jnp.float32)
    input_grad = place_terms(tap_terms, channels, out_depth + 1, out_rows, out_cols, planes, rows, cols)
    return (input_grad, weight_grad)
```

```python
import math

import jax
import jax.numpy as jnp
from jax import lax
from jax.experimental import pallas as pl
from jax.experimental.pallas import tpu as pltpu
from jax.sharding import PartitionSpec as P

F32 = jnp.float32
BF16 = jnp.bfloat16
PARAMS = pltpu.CompilerParams(vmem_limit_bytes=48 * 1024 * 1024)


def shifted(value, axis, steps):
    count = lax.axis_size(axis)
    leading, last = (max(0, -steps), min(count, count - steps))
    return lax.ppermute(value, axis, [(source, source + steps) for source in range(leading, last)])


def swapped(value, axis, bits):
    count = lax.axis_size(axis)
    return lax.ppermute(value, axis, [(source, source ^ bits) for source in range(count)])


def halves(value):
    high = value.astype(BF16)
    return high, (value - high.astype(F32)).astype(BF16)


def dot(a, b):
    return lax.dot_general(a, b, (((1,), (0,)), ((), ())), preferred_element_type=F32)


def dot_t(a, b):
    return lax.dot_general(a, b, (((1,), (1,)), ((), ())), preferred_element_type=F32)


def column_taps(cols, out_cols):
    x = lax.broadcasted_iota(jnp.int32, (cols, 3 * out_cols), 0)
    c = lax.broadcasted_iota(jnp.int32, (cols, 3 * out_cols), 1)
    dx = c // out_cols
    return jnp.where(x == 2 * (c - dx * out_cols) + dx - 1, 1.0, 0.0).astype(BF16)


def split_columns(v_ref, planes, rows, channels, taps, high_ref, low_ref, x_high, x_low, lanes):
    for h in range(v_ref.shape[1] // 128):
        lanes[...] = v_ref[:, h * 128 : (h + 1) * 128]
        for k in range(planes * rows):
            high, low = halves(lanes[pl.ds(k, channels, stride=planes * rows), :])
            x_high[k * channels : (k + 1) * channels, h * 128 : (h + 1) * 128] = high
            x_low[k * channels : (k + 1) * channels, h * 128 : (h + 1) * 128] = low
    high_ref[...] = dot(x_high[...], taps).astype(BF16)
    low_ref[...] = dot(x_low[...], taps).astype(BF16)


def prepare(volume, out_cols):
    channels, planes, rows, cols = volume.shape
    count = planes * rows * channels

    def kernel(v_ref, high_ref, low_ref, *scratch):
        split_columns(v_ref, planes, rows, channels, column_taps(cols, out_cols), high_ref, low_ref, *scratch)

    return pl.pallas_call(
        kernel,
        out_shape=[jax.ShapeDtypeStruct((count, 3 * out_cols), BF16)] * 2,
        scratch_shapes=[pltpu.VMEM((count, cols), BF16)] * 2 + [pltpu.VMEM((count, 128), F32)],
        compiler_params=PARAMS,
        name="prepare",
    )(volume.reshape(-1, cols))


def weight_partial(high, low, rim, grads, parts):
    channels, _, rows, cols = rim.shape
    filters, _, out_rows, out_cols = grads[0].shape
    groups = len(grads)
    cells = out_rows * out_cols
    width = 27 * channels
    block = filters // parts

    def kernel(*refs):
        high_ref, low_ref, rim_ref = refs[:3]
        g_refs = refs[3 : 3 + groups]
        out_refs = refs[3 + groups : 3 + groups + parts]
        r_high, r_low, x_high, x_low, lanes, g_both, b_high, b_low, total = refs[3 + groups + parts :]
        split_columns(rim_ref, 1, rows, channels, column_taps(cols, out_cols), r_high, r_low, x_high, x_low, lanes)
        for j in range(groups):
            for q in range(out_rows):
                upper, lower = halves(g_refs[j][pl.ds(q, filters, stride=out_rows), :])
                g_both[j * filters : (j + 1) * filters, q * out_cols : (q + 1) * out_cols] = upper
                g_both[(groups + j) * filters : (groups + j + 1) * filters, q * out_cols : (q + 1) * out_cols] = lower
        for source, other, target in ((high_ref, r_high, b_high), (low_ref, r_low, b_low)):
            for dz in range(3):
                for dy in range(3):
                    for q in range(out_rows):
                        y = 2 * q + dy - 1
                        for dx in range(3):
                            at = ((dz * 3 + dy) * 3 + dx) * channels
                            if y < 0:
                                piece = jnp.zeros((channels, out_cols), BF16)
                            elif dz == 0:
                                piece = other[y * channels : (y + 1) * channels, dx * out_cols : (dx + 1) * out_cols]
                            else:
                                first = ((dz - 1) * rows + y) * channels
                                piece = source[first : first + channels, dx * out_cols : (dx + 1) * out_cols]
                            target[at : at + channels, q * out_cols : (q + 1) * out_cols] = piece
        count = groups * filters
        both = dot_t(g_both[...], b_high[...])
        total[...] = both[:count] + both[count:] + dot_t(g_both[:count, :], b_low[...])
        slab = lax.axis_index("gz")
        for k in range(parts):
            for j in range(groups):
                first = pl.multiple_of(j * filters + (slab ^ k) * block, 8)
                out_refs[k][j * block : (j + 1) * block, :] = total[pl.ds(first, block), :]

    return pl.pallas_call(
        kernel,
        out_shape=[jax.ShapeDtypeStruct((groups * block, width), F32)] * parts,
        scratch_shapes=[
            pltpu.VMEM((rows * channels, 3 * out_cols), BF16),
            pltpu.VMEM((rows * channels, 3 * out_cols), BF16),
            pltpu.VMEM((rows * channels, cols), BF16),
            pltpu.VMEM((rows * channels, cols), BF16),
            pltpu.VMEM((rows * channels, 128), F32),
            pltpu.VMEM((2 * groups * filters, cells), BF16),
            pltpu.VMEM((width, cells), BF16),
            pltpu.VMEM((width, cells), BF16),
            pltpu.VMEM((groups * filters, width), F32),
        ],
        compiler_params=PARAMS,
        name="weight_partial",
    )(high, low, rim.reshape(-1, cols), *[g.reshape(-1, out_cols) for g in grads])


def add_slabs(pieces, groups):
    rows, width = pieces[0].shape
    block = rows // groups
    parts = len(pieces)

    def kernel(*refs):
        for j in range(groups):
            value = refs[0][j * block : (j + 1) * block, :]
            for k in range(1, parts):
                value = value + refs[k][j * block : (j + 1) * block, :]
            refs[parts + j][...] = value

    return pl.pallas_call(
        kernel,
        out_shape=[jax.ShapeDtypeStruct((block, width), F32)] * groups,
        compiler_params=PARAMS,
        name="add_slabs",
    )(*pieces)


def weave_channels(pieces, channels, factor):
    groups = len(pieces)
    block, width = pieces[0].shape
    total = groups * channels
    span = 128
    taps = span // channels
    chunks = -(-width // span)

    def kernel(*refs):
        me = lax.axis_index("af")
        row = lax.broadcasted_iota(jnp.int32, (groups * span, taps * total), 0)
        col = lax.broadcasted_iota(jnp.int32, (groups * span, taps * total), 1)
        j = row // span
        inner = row - j * span
        tap = inner // channels
        place = jnp.where(col == tap * total + (j ^ me) * channels + (inner - tap * channels), 1.0, 0.0).astype(BF16)
        for c in range(chunks):
            size = min(span, width - c * span)
            columns = []
            for j in range(groups):
                value = refs[j][:, c * span : c * span + size] * factor
                if size < span:
                    value = jnp.concatenate([value, jnp.zeros((block, span - size), F32)], axis=1)
                columns.append(value)
            wide = jnp.concatenate(columns, axis=1)
            high = wide.astype(BF16).astype(F32)
            rest = wide - high
            middle = rest.astype(BF16).astype(F32)
            stacked = jnp.concatenate([high, middle, rest - middle], axis=0).astype(BF16)
            woven = dot(stacked, place)
            result = woven[:block] + woven[block : 2 * block] + woven[2 * block :]
            first = c * taps * total
            last = min(first + taps * total, 27 * total)
            refs[groups][:, first:last] = result[:, : last - first]

    return pl.pallas_call(
        kernel,
        out_shape=jax.ShapeDtypeStruct((block, 27 * total), F32),
        compiler_params=PARAMS,
        name="weave_channels",
    )(*pieces)


def stack_slabs(pieces):
    block, width = pieces[0].shape
    parts = len(pieces)

    def kernel(*refs):
        slab = lax.axis_index("gz")
        for k in range(parts):
            refs[parts][slab ^ k] = refs[k][...]

    return pl.pallas_call(
        kernel,
        out_shape=jax.ShapeDtypeStruct((parts, block, width), F32),
        compiler_params=PARAMS,
        name="stack_slabs",
    )(*pieces).reshape(parts * block, width)


def input_gradient(weights, grads, uppers, volume_shape):
    channels, planes, rows, cols = volume_shape
    groups = len(grads)
    filters, _, out_rows, out_cols = grads[0].shape
    count = groups * filters
    cells = out_rows * out_cols
    total = weights[0].shape[1] // 27
    padded = -(-27 * total // 128) * 128
    third = 9 * channels

    def kernel(*refs):
        w_refs, g_refs, u_refs = refs[:groups], refs[groups : 2 * groups], refs[2 * groups : 3 * groups]
        out_ref = refs[3 * groups]
        turned, a_high, a_low, g_high, g_low, t_even, t_odd, woven, lanes = refs[3 * groups + 1 :]
        for first in range(0, padded, 128):
            size = min(128, 27 * total - first)
            value = jnp.concatenate([w[:, first : first + size] for w in w_refs], axis=0)
            if size < 128:
                value = jnp.concatenate([value, jnp.zeros((count, 128 - size), F32)], axis=1)
            turned[first : first + 128, :] = value.T
        me = lax.axis_index("af")
        for tap in range(27):
            first = pl.multiple_of(tap * total + me * channels, 8)
            high, low = halves(turned[pl.ds(first, channels), :])
            a_high[tap * channels : (tap + 1) * channels, :] = high
            a_low[tap * channels : (tap + 1) * channels, :] = low
        for side, source in enumerate((g_refs, u_refs)):
            for j in range(groups):
                for q in range(out_rows):
                    high, low = halves(source[j][pl.ds(q, filters, stride=out_rows), :])
                    at = side * count + j * filters
                    g_high[at : at + filters, q * out_cols : (q + 1) * out_cols] = high
                    g_low[at : at + filters, q * out_cols : (q + 1) * out_cols] = low
        e_high, e_low = a_high[third : 2 * third, :], a_low[third : 2 * third, :]
        both = jnp.concatenate([e_high, e_low], axis=1)
        own_high = g_high[:count, :]
        t_even[...] = dot(both, jnp.concatenate([own_high, own_high], axis=0)) + dot(e_high, g_low[:count, :])
        o_high = jnp.concatenate([a_high[2 * third :, :], a_high[:third, :]], axis=1)
        o_low = jnp.concatenate([a_low[2 * third :, :], a_low[:third, :]], axis=1)
        t_odd[...] = dot(o_high, g_high[...]) + dot(o_high, g_low[...]) + dot(o_low, g_high[...])
        for z, terms in enumerate((t_even, t_odd)):
            for y in range(rows):
                q = y // 2
                for dx in range(3):
                    def term(dy, at):
                        first = (dy * 3 + dx) * channels
                        return terms[first : first + channels, at * out_cols : (at + 1) * out_cols]

                    if y % 2 == 0:
                        value = term(1, q)
                    else:
                        value = term(2, q)
                        if q + 1 < out_rows:
                            value = value + term(0, q + 1)
                    high, low = halves(value)
                    first = (z * rows + y) * channels
                    woven[first : first + channels, dx * out_cols : (dx + 1) * out_cols] = high
                    woven[first : first + channels, (3 + dx) * out_cols : (4 + dx) * out_cols] = low
        taps = column_taps(cols, out_cols)
        result = dot_t(woven[...], jnp.concatenate([taps, taps], axis=1))
        for h in range(cols // 128):
            for k in range(planes * rows):
                piece = result[k * channels : (k + 1) * channels, h * 128 : (h + 1) * 128]
                lanes[pl.ds(k, channels, stride=planes * rows), :] = piece
            out_ref[:, h * 128 : (h + 1) * 128] = lanes[...]

    return pl.pallas_call(
        kernel,
        out_shape=jax.ShapeDtypeStruct((channels * planes * rows, cols), F32),
        scratch_shapes=[
            pltpu.VMEM((padded, count), F32),
            pltpu.VMEM((27 * channels, count), BF16),
            pltpu.VMEM((27 * channels, count), BF16),
            pltpu.VMEM((2 * count, cells), BF16),
            pltpu.VMEM((2 * count, cells), BF16),
            pltpu.VMEM((third, cells), F32),
            pltpu.VMEM((third, cells), F32),
            pltpu.VMEM((planes * rows * channels, 6 * out_cols), BF16),
            pltpu.VMEM((planes * rows * channels, 128), F32),
        ],
        compiler_params=PARAMS,
        name="input_gradient",
    )(
        *weights,
        *[g.reshape(-1, out_cols) for g in grads],
        *[u.reshape(-1, out_cols) for u in uppers],
    ).reshape(volume_shape)


def spread(value):
    step = lax.axis_size("af") // 2
    have = {0: value}
    while step:
        for j in list(have):
            have[j ^ step] = swapped(have[j], "af", step)
        step //= 2
    return [have[j] for j in range(lax.axis_size("af"))]


def fast(volume, out_grad, weight):
    channels, planes, rows, cols = volume.shape
    filters, out_depth, out_rows, out_cols = out_grad.shape
    parts, groups = lax.axis_size("gz"), lax.axis_size("af")
    factor = 1.0 / math.sqrt(out_depth * parts * out_rows * out_cols)
    grads = spread(out_grad)
    rim = shifted(volume[:, planes - 1 : planes], "gz", 1)
    uppers = spread(shifted(out_grad, "gz", -1))
    weights = spread(weight)
    high, low = prepare(volume, out_cols)
    sent = weight_partial(high, low, rim, grads, parts)
    arrived = [sent[0]] + [swapped(sent[k], "gz", k) for k in range(1, parts)]
    sums = add_slabs(arrived, groups)
    crossed = [sums[0]] + [swapped(sums[j], "af", j) for j in range(1, groups)]
    own = weave_channels(crossed, channels, factor)
    weight_grad = stack_slabs([own] + [swapped(own, "gz", k) for k in range(1, parts)])
    input_grad = input_gradient(weights, grads, uppers, volume.shape)
    return (input_grad, weight_grad)


def tap_matrix(extended, out_depth, out_rows, out_cols):
    channels = extended.shape[0]
    padded = jnp.pad(extended, ((0, 0), (0, 1), (1, 1), (1, 1)))
    split = padded.reshape(channels, out_depth + 1, 2, out_rows + 1, 2, out_cols + 1, 2)
    pieces = []
    for depth_tap in range(3):
        for row_tap in range(3):
            for col_tap in range(3):
                dz_lo = depth_tap // 2
                dy_lo = row_tap // 2
                dx_lo = col_tap // 2
                pieces.append(
                    split[
                        :,
                        dz_lo : dz_lo + out_depth,
                        depth_tap % 2,
                        dy_lo : dy_lo + out_rows,
                        row_tap % 2,
                        dx_lo : dx_lo + out_cols,
                        col_tap % 2,
                    ]
                )
    stacked = jnp.stack(pieces, axis=0)
    return stacked.reshape(27 * channels, out_depth * out_rows * out_cols)


def place_terms(tap_terms, channels, depth_count, out_rows, out_cols, planes, rows, cols):
    shaped = tap_terms.reshape(27, channels, depth_count, out_rows, out_cols)
    phases = {}
    for depth_tap in range(3):
        for row_tap in range(3):
            for col_tap in range(3):
                index = 9 * depth_tap + 3 * row_tap + col_tap
                dz_lo = depth_tap // 2
                dy_lo = row_tap // 2
                dx_lo = col_tap // 2
                moved = jnp.pad(
                    shaped[index],
                    ((0, 0), (dz_lo, 1 - dz_lo), (dy_lo, 1 - dy_lo), (dx_lo, 1 - dx_lo)),
                )
                parity = (depth_tap % 2, row_tap % 2, col_tap % 2)
                phases[parity] = moved if parity not in phases else phases[parity] + moved
    depth_pairs = []
    for depth_bit in range(2):
        row_pairs = []
        for row_bit in range(2):
            col_pair = jnp.stack(
                [phases[depth_bit, row_bit, 0], phases[depth_bit, row_bit, 1]], axis=-1
            )
            row_pairs.append(col_pair)
        depth_pairs.append(jnp.stack(row_pairs, axis=3))
    woven = jnp.stack(depth_pairs, axis=2)
    canvas = woven.reshape(channels, 2 * (depth_count + 1), 2 * (out_rows + 1), 2 * (out_cols + 1))
    return canvas[:, 1 : planes + 1, 1 : rows + 1, 1 : cols + 1]


def general(volume, out_grad, weight):
    channels, planes, rows, cols = volume.shape
    filters, out_depth, out_rows, out_cols = out_grad.shape
    in_total = weight.shape[1] // 27
    factor = 1.0 / math.sqrt(out_depth * lax.axis_size("gz") * out_rows * out_cols)
    lower_rim = shifted(volume[:, planes - 1 : planes], "gz", 1)
    extended = jnp.concatenate([lower_rim, volume], axis=1)
    upper_rim = shifted(out_grad, "gz", -1)
    grad_ext = jnp.concatenate([out_grad, upper_rim], axis=1)
    grads_all, weight_all = (
        lax.all_gather(grad_ext, "af", axis=0, tiled=True),
        lax.all_gather(weight, "af", axis=0, tiled=True),
    )
    all_filters = grads_all.shape[0]
    channel_first = lax.axis_index("af") * channels
    weight_cube = weight_all.reshape(all_filters, 27, in_total)
    own_weight = lax.dynamic_slice_in_dim(weight_cube, channel_first, channels, 2).reshape(
        all_filters, 27 * channels
    )
    tap_terms = lax.dot_general(
        own_weight,
        grads_all.reshape(all_filters, -1),
        (((0,), (0,)), ((), ())),
        precision=lax.Precision.HIGHEST,
        preferred_element_type=jnp.float32,
    )
    input_grad = place_terms(
        tap_terms, channels, out_depth + 1, out_rows, out_cols, planes, rows, cols
    )
    local_grads = out_grad.reshape(filters, -1)
    portion = lax.all_gather(extended, "af", axis=0, tiled=True)
    count = portion.shape[0]
    tap_rows = tap_matrix(portion, out_depth, out_rows, out_cols)
    partial_grad = lax.dot_general(
        local_grads,
        tap_rows,
        (((1,), (1,)), ((), ())),
        precision=lax.Precision.HIGHEST,
        preferred_element_type=jnp.float32,
    )
    partial_grad = partial_grad.reshape(filters, 27, count)
    summed = lax.psum(partial_grad, "gz")
    weight_grad = (summed * factor).reshape(filters, 27 * in_total)
    return (input_grad, weight_grad)


def local(volume, out_grad, weight):
    channels, planes, rows, _ = volume.shape
    filters, out_depth, out_rows, _ = out_grad.shape
    parts, groups = lax.axis_size("gz"), lax.axis_size("af")
    powers = parts & (parts - 1) == 0 and groups & (groups - 1) == 0
    whole_tiles = channels % 16 == 0 and filters % (8 * parts) == 0 and filters * groups == 128
    if powers and whole_tiles and out_depth == 1:
        return fast(volume, out_grad, weight)
    return general(volume, out_grad, weight)


def solution(mesh):
    return jax.shard_map(
        local,
        mesh=mesh,
        in_specs=(
            P("af", ("grp", "gz"), None, None),
            P("af", ("grp", "gz"), None, None),
            P("af", None),
        ),
        out_specs=(P("af", ("grp", "gz"), None, None), P("af", "grp")),
        check_vma=False,
    )
```

```python
import math

import jax
import jax.numpy as jnp
from jax import lax
from jax.experimental import pallas as pl
from jax.experimental.pallas import tpu as pltpu
from jax.sharding import PartitionSpec as P

F32 = jnp.float32
BF16 = jnp.bfloat16
PARAMS = pltpu.CompilerParams(vmem_limit_bytes=48 * 1024 * 1024)


def shifted(value, axis, steps):
    count = lax.axis_size(axis)
    leading, last = (max(0, -steps), min(count, count - steps))
    return lax.ppermute(value, axis, [(source, source + steps) for source in range(leading, last)])


def swapped(value, axis, bits):
    count = lax.axis_size(axis)
    return lax.ppermute(value, axis, [(source, source ^ bits) for source in range(count)])


def halves(value):
    high = value.astype(BF16)
    return high, (value - high.astype(F32)).astype(BF16)


def dot(a, b):
    return lax.dot_general(a, b, (((1,), (0,)), ((), ())), preferred_element_type=F32)


def dot_t(a, b):
    return lax.dot_general(a, b, (((1,), (1,)), ((), ())), preferred_element_type=F32)


def column_taps(cols, out_cols):
    x = lax.broadcasted_iota(jnp.int32, (cols, 3 * out_cols), 0)
    c = lax.broadcasted_iota(jnp.int32, (cols, 3 * out_cols), 1)
    dx = c // out_cols
    return jnp.where(x == 2 * (c - dx * out_cols) + dx - 1, 1.0, 0.0).astype(BF16)


def split_columns(v_ref, planes, rows, channels, taps, high_ref, low_ref, x_high, x_low, lanes):
    for h in range(v_ref.shape[1] // 128):
        lanes[...] = v_ref[:, h * 128 : (h + 1) * 128]
        for k in range(planes * rows):
            high, low = halves(lanes[pl.ds(k, channels, stride=planes * rows), :])
            x_high[k * channels : (k + 1) * channels, h * 128 : (h + 1) * 128] = high
            x_low[k * channels : (k + 1) * channels, h * 128 : (h + 1) * 128] = low
    high_ref[...] = dot(x_high[...], taps).astype(BF16)
    low_ref[...] = dot(x_low[...], taps).astype(BF16)


def prepare(volume, out_cols):
    channels, planes, rows, cols = volume.shape
    count = planes * rows * channels

    def kernel(v_ref, high_ref, low_ref, *scratch):
        split_columns(v_ref, planes, rows, channels, column_taps(cols, out_cols), high_ref, low_ref, *scratch)

    return pl.pallas_call(
        kernel,
        out_shape=[jax.ShapeDtypeStruct((count, 3 * out_cols), BF16)] * 2,
        scratch_shapes=[pltpu.VMEM((count, cols), BF16)] * 2 + [pltpu.VMEM((count, 128), F32)],
        compiler_params=PARAMS,
        name="prepare",
    )(volume.reshape(-1, cols))


def weight_partial(high, low, rim, grads, parts):
    channels, _, rows, cols = rim.shape
    filters, _, out_rows, out_cols = grads[0].shape
    groups = len(grads)
    cells = out_rows * out_cols
    width = 27 * channels
    block = filters // parts

    def kernel(*refs):
        high_ref, low_ref, rim_ref = refs[:3]
        g_refs = refs[3 : 3 + groups]
        out_refs = refs[3 + groups : 3 + groups + parts]
        r_high, r_low, x_high, x_low, lanes, g_both, b_high, b_low, total = refs[3 + groups + parts :]
        split_columns(rim_ref, 1, rows, channels, column_taps(cols, out_cols), r_high, r_low, x_high, x_low, lanes)
        for j in range(groups):
            for q in range(out_rows):
                upper, lower = halves(g_refs[j][pl.ds(q, filters, stride=out_rows), :])
                g_both[j * filters : (j + 1) * filters, q * out_cols : (q + 1) * out_cols] = upper
                g_both[(groups + j) * filters : (groups + j + 1) * filters, q * out_cols : (q + 1) * out_cols] = lower
        for source, other, target in ((high_ref, r_high, b_high), (low_ref, r_low, b_low)):
            for dz in range(3):
                for dy in range(3):
                    for q in range(out_rows):
                        y = 2 * q + dy - 1
                        for dx in range(3):
                            at = ((dz * 3 + dy) * 3 + dx) * channels
                            if y < 0:
                                piece = jnp.zeros((channels, out_cols), BF16)
                            elif dz == 0:
                                piece = other[y * channels : (y + 1) * channels, dx * out_cols : (dx + 1) * out_cols]
                            else:
                                first = ((dz - 1) * rows + y) * channels
                                piece = source[first : first + channels, dx * out_cols : (dx + 1) * out_cols]
                            target[at : at + channels, q * out_cols : (q + 1) * out_cols] = piece
        count = groups * filters
        both = dot_t(g_both[...], b_high[...])
        total[...] = both[:count] + both[count:] + dot_t(g_both[:count, :], b_low[...])
        slab = lax.axis_index("gz")
        for k in range(parts):
            for j in range(groups):
                first = pl.multiple_of(j * filters + (slab ^ k) * block, 8)
                out_refs[k][j * block : (j + 1) * block, :] = total[pl.ds(first, block), :]

    return pl.pallas_call(
        kernel,
        out_shape=[jax.ShapeDtypeStruct((groups * block, width), F32)] * parts,
        scratch_shapes=[
            pltpu.VMEM((rows * channels, 3 * out_cols), BF16),
            pltpu.VMEM((rows * channels, 3 * out_cols), BF16),
            pltpu.VMEM((rows * channels, cols), BF16),
            pltpu.VMEM((rows * channels, cols), BF16),
            pltpu.VMEM((rows * channels, 128), F32),
            pltpu.VMEM((2 * groups * filters, cells), BF16),
            pltpu.VMEM((width, cells), BF16),
            pltpu.VMEM((width, cells), BF16),
            pltpu.VMEM((groups * filters, width), F32),
        ],
        compiler_params=PARAMS,
        name="weight_partial",
    )(high, low, rim.reshape(-1, cols), *[g.reshape(-1, out_cols) for g in grads])


def add_slabs(pieces, groups):
    rows, width = pieces[0].shape
    block = rows // groups
    parts = len(pieces)

    def kernel(*refs):
        for j in range(groups):
            value = refs[0][j * block : (j + 1) * block, :]
            for k in range(1, parts):
                value = value + refs[k][j * block : (j + 1) * block, :]
            refs[parts + j][...] = value

    return pl.pallas_call(
        kernel,
        out_shape=[jax.ShapeDtypeStruct((block, width), F32)] * groups,
        compiler_params=PARAMS,
        name="add_slabs",
    )(*pieces)


def weave_channels(pieces, channels, factor):
    groups = len(pieces)
    block, width = pieces[0].shape
    total = groups * channels
    span = 128
    taps = span // channels
    chunks = -(-width // span)

    def kernel(*refs):
        me = lax.axis_index("af")
        row = lax.broadcasted_iota(jnp.int32, (groups * span, taps * total), 0)
        col = lax.broadcasted_iota(jnp.int32, (groups * span, taps * total), 1)
        j = row // span
        inner = row - j * span
        tap = inner // channels
        place = jnp.where(col == tap * total + (j ^ me) * channels + (inner - tap * channels), 1.0, 0.0).astype(BF16)
        for c in range(chunks):
            size = min(span, width - c * span)
            columns = []
            for j in range(groups):
                value = refs[j][:, c * span : c * span + size] * factor
                if size < span:
                    value = jnp.concatenate([value, jnp.zeros((block, span - size), F32)], axis=1)
                columns.append(value)
            wide = jnp.concatenate(columns, axis=1)
            high = wide.astype(BF16).astype(F32)
            rest = wide - high
            middle = rest.astype(BF16).astype(F32)
            stacked = jnp.concatenate([high, middle, rest - middle], axis=0).astype(BF16)
            woven = dot(stacked, place)
            result = woven[:block] + woven[block : 2 * block] + woven[2 * block :]
            first = c * taps * total
            last = min(first + taps * total, 27 * total)
            refs[groups][:, first:last] = result[:, : last - first]

    return pl.pallas_call(
        kernel,
        out_shape=jax.ShapeDtypeStruct((block, 27 * total), F32),
        compiler_params=PARAMS,
        name="weave_channels",
    )(*pieces)


def stack_slabs(pieces):
    block, width = pieces[0].shape
    parts = len(pieces)

    def kernel(*refs):
        slab = lax.axis_index("gz")
        for k in range(parts):
            refs[parts][slab ^ k] = refs[k][...]

    return pl.pallas_call(
        kernel,
        out_shape=jax.ShapeDtypeStruct((parts, block, width), F32),
        compiler_params=PARAMS,
        name="stack_slabs",
    )(*pieces).reshape(parts * block, width)


def input_gradient(weights, grads, uppers, volume_shape):
    channels, planes, rows, cols = volume_shape
    groups = len(grads)
    filters, _, out_rows, out_cols = grads[0].shape
    count = groups * filters
    cells = out_rows * out_cols
    total = weights[0].shape[1] // 27
    padded = -(-27 * total // 128) * 128
    third = 9 * channels

    def kernel(*refs):
        w_refs, g_refs, u_refs = refs[:groups], refs[groups : 2 * groups], refs[2 * groups : 3 * groups]
        out_ref = refs[3 * groups]
        turned, a_high, a_low, g_high, g_low, t_even, t_odd, woven, lanes = refs[3 * groups + 1 :]
        for first in range(0, padded, 128):
            size = min(128, 27 * total - first)
            value = jnp.concatenate([w[:, first : first + size] for w in w_refs], axis=0)
            if size < 128:
                value = jnp.concatenate([value, jnp.zeros((count, 128 - size), F32)], axis=1)
            turned[first : first + 128, :] = value.T
        me = lax.axis_index("af")
        for tap in range(27):
            first = pl.multiple_of(tap * total + me * channels, 8)
            high, low = halves(turned[pl.ds(first, channels), :])
            a_high[tap * channels : (tap + 1) * channels, :] = high
            a_low[tap * channels : (tap + 1) * channels, :] = low
        for side, source in enumerate((g_refs, u_refs)):
            for j in range(groups):
                for q in range(out_rows):
                    high, low = halves(source[j][pl.ds(q, filters, stride=out_rows), :])
                    at = side * count + j * filters
                    g_high[at : at + filters, q * out_cols : (q + 1) * out_cols] = high
                    g_low[at : at + filters, q * out_cols : (q + 1) * out_cols] = low
        e_high, e_low = a_high[third : 2 * third, :], a_low[third : 2 * third, :]
        both = jnp.concatenate([e_high, e_low], axis=1)
        own_high = g_high[:count, :]
        t_even[...] = dot(both, jnp.concatenate([own_high, own_high], axis=0)) + dot(e_high, g_low[:count, :])
        o_high = jnp.concatenate([a_high[2 * third :, :], a_high[:third, :]], axis=1)
        o_low = jnp.concatenate([a_low[2 * third :, :], a_low[:third, :]], axis=1)
        t_odd[...] = dot(o_high, g_high[...]) + dot(o_high, g_low[...]) + dot(o_low, g_high[...])
        for z, terms in enumerate((t_even, t_odd)):
            for y in range(rows):
                q = y // 2
                for dx in range(3):
                    def term(dy, at):
                        first = (dy * 3 + dx) * channels
                        return terms[first : first + channels, at * out_cols : (at + 1) * out_cols]

                    if y % 2 == 0:
                        value = term(1, q)
                    else:
                        value = term(2, q)
                        if q + 1 < out_rows:
                            value = value + term(0, q + 1)
                    high, low = halves(value)
                    first = (z * rows + y) * channels
                    woven[first : first + channels, dx * out_cols : (dx + 1) * out_cols] = high
                    woven[first : first + channels, (3 + dx) * out_cols : (4 + dx) * out_cols] = low
        taps = column_taps(cols, out_cols)
        result = dot_t(woven[...], jnp.concatenate([taps, taps], axis=1))
        for h in range(cols // 128):
            for k in range(planes * rows):
                piece = result[k * channels : (k + 1) * channels, h * 128 : (h + 1) * 128]
                lanes[pl.ds(k, channels, stride=planes * rows), :] = piece
            out_ref[:, h * 128 : (h + 1) * 128] = lanes[...]

    return pl.pallas_call(
        kernel,
        out_shape=jax.ShapeDtypeStruct((channels * planes * rows, cols), F32),
        scratch_shapes=[
            pltpu.VMEM((padded, count), F32),
            pltpu.VMEM((27 * channels, count), BF16),
            pltpu.VMEM((27 * channels, count), BF16),
            pltpu.VMEM((2 * count, cells), BF16),
            pltpu.VMEM((2 * count, cells), BF16),
            pltpu.VMEM((third, cells), F32),
            pltpu.VMEM((third, cells), F32),
            pltpu.VMEM((planes * rows * channels, 6 * out_cols), BF16),
            pltpu.VMEM((planes * rows * channels, 128), F32),
        ],
        compiler_params=PARAMS,
        name="input_gradient",
    )(
        *weights,
        *[g.reshape(-1, out_cols) for g in grads],
        *[u.reshape(-1, out_cols) for u in uppers],
    ).reshape(volume_shape)


def spread(value):
    step = lax.axis_size("af") // 2
    have = {0: value}
    while step:
        for j in list(have):
            have[j ^ step] = swapped(have[j], "af", step)
        step //= 2
    return [have[j] for j in range(lax.axis_size("af"))]


def fast(volume, out_grad, weight):
    channels, planes, rows, cols = volume.shape
    filters, out_depth, out_rows, out_cols = out_grad.shape
    parts, groups = lax.axis_size("gz"), lax.axis_size("af")
    factor = 1.0 / math.sqrt(out_depth * parts * out_rows * out_cols)
    grads = spread(out_grad)
    rim = shifted(volume[:, planes - 1 : planes], "gz", 1)
    uppers = spread(shifted(out_grad, "gz", -1))
    weights = spread(weight)
    high, low = prepare(volume, out_cols)
    sent = weight_partial(high, low, rim, grads, parts)
    arrived = [sent[0]] + [swapped(sent[k], "gz", k) for k in range(1, parts)]
    input_grad = input_gradient(weights, grads, uppers, volume.shape)
    input_grad, arrived = lax.optimization_barrier((input_grad, arrived))
    sums = add_slabs(arrived, groups)
    crossed = [sums[0]] + [swapped(sums[j], "af", j) for j in range(1, groups)]
    own = weave_channels(crossed, channels, factor)
    weight_grad = stack_slabs([own] + [swapped(own, "gz", k) for k in range(1, parts)])
    return (input_grad, weight_grad)


def tap_matrix(extended, out_depth, out_rows, out_cols):
    channels = extended.shape[0]
    padded = jnp.pad(extended, ((0, 0), (0, 1), (1, 1), (1, 1)))
    split = padded.reshape(channels, out_depth + 1, 2, out_rows + 1, 2, out_cols + 1, 2)
    pieces = []
    for depth_tap in range(3):
        for row_tap in range(3):
            for col_tap in range(3):
                dz_lo = depth_tap // 2
                dy_lo = row_tap // 2
                dx_lo = col_tap // 2
                pieces.append(
                    split[
                        :,
                        dz_lo : dz_lo + out_depth,
                        depth_tap % 2,
                        dy_lo : dy_lo + out_rows,
                        row_tap % 2,
                        dx_lo : dx_lo + out_cols,
                        col_tap % 2,
                    ]
                )
    stacked = jnp.stack(pieces, axis=0)
    return stacked.reshape(27 * channels, out_depth * out_rows * out_cols)


def place_terms(tap_terms, channels, depth_count, out_rows, out_cols, planes, rows, cols):
    shaped = tap_terms.reshape(27, channels, depth_count, out_rows, out_cols)
    phases = {}
    for depth_tap in range(3):
        for row_tap in range(3):
            for col_tap in range(3):
                index = 9 * depth_tap + 3 * row_tap + col_tap
                dz_lo = depth_tap // 2
                dy_lo = row_tap // 2
                dx_lo = col_tap // 2
                moved = jnp.pad(
                    shaped[index],
                    ((0, 0), (dz_lo, 1 - dz_lo), (dy_lo, 1 - dy_lo), (dx_lo, 1 - dx_lo)),
                )
                parity = (depth_tap % 2, row_tap % 2, col_tap % 2)
                phases[parity] = moved if parity not in phases else phases[parity] + moved
    depth_pairs = []
    for depth_bit in range(2):
        row_pairs = []
        for row_bit in range(2):
            col_pair = jnp.stack(
                [phases[depth_bit, row_bit, 0], phases[depth_bit, row_bit, 1]], axis=-1
            )
            row_pairs.append(col_pair)
        depth_pairs.append(jnp.stack(row_pairs, axis=3))
    woven = jnp.stack(depth_pairs, axis=2)
    canvas = woven.reshape(channels, 2 * (depth_count + 1), 2 * (out_rows + 1), 2 * (out_cols + 1))
    return canvas[:, 1 : planes + 1, 1 : rows + 1, 1 : cols + 1]


def general(volume, out_grad, weight):
    channels, planes, rows, cols = volume.shape
    filters, out_depth, out_rows, out_cols = out_grad.shape
    in_total = weight.shape[1] // 27
    factor = 1.0 / math.sqrt(out_depth * lax.axis_size("gz") * out_rows * out_cols)
    lower_rim = shifted(volume[:, planes - 1 : planes], "gz", 1)
    extended = jnp.concatenate([lower_rim, volume], axis=1)
    upper_rim = shifted(out_grad, "gz", -1)
    grad_ext = jnp.concatenate([out_grad, upper_rim], axis=1)
    grads_all, weight_all = (
        lax.all_gather(grad_ext, "af", axis=0, tiled=True),
        lax.all_gather(weight, "af", axis=0, tiled=True),
    )
    all_filters = grads_all.shape[0]
    channel_first = lax.axis_index("af") * channels
    weight_cube = weight_all.reshape(all_filters, 27, in_total)
    own_weight = lax.dynamic_slice_in_dim(weight_cube, channel_first, channels, 2).reshape(
        all_filters, 27 * channels
    )
    tap_terms = lax.dot_general(
        own_weight,
        grads_all.reshape(all_filters, -1),
        (((0,), (0,)), ((), ())),
        precision=lax.Precision.HIGHEST,
        preferred_element_type=jnp.float32,
    )
    input_grad = place_terms(
        tap_terms, channels, out_depth + 1, out_rows, out_cols, planes, rows, cols
    )
    local_grads = out_grad.reshape(filters, -1)
    portion = lax.all_gather(extended, "af", axis=0, tiled=True)
    count = portion.shape[0]
    tap_rows = tap_matrix(portion, out_depth, out_rows, out_cols)
    partial_grad = lax.dot_general(
        local_grads,
        tap_rows,
        (((1,), (1,)), ((), ())),
        precision=lax.Precision.HIGHEST,
        preferred_element_type=jnp.float32,
    )
    partial_grad = partial_grad.reshape(filters, 27, count)
    summed = lax.psum(partial_grad, "gz")
    weight_grad = (summed * factor).reshape(filters, 27 * in_total)
    return (input_grad, weight_grad)


def local(volume, out_grad, weight):
    channels, planes, rows, _ = volume.shape
    filters, out_depth, out_rows, _ = out_grad.shape
    parts, groups = lax.axis_size("gz"), lax.axis_size("af")
    powers = parts & (parts - 1) == 0 and groups & (groups - 1) == 0
    whole_tiles = channels % 16 == 0 and filters % (8 * parts) == 0 and filters * groups == 128
    if powers and whole_tiles and out_depth == 1:
        return fast(volume, out_grad, weight)
    return general(volume, out_grad, weight)


def solution(mesh):
    return jax.shard_map(
        local,
        mesh=mesh,
        in_specs=(
            P("af", ("grp", "gz"), None, None),
            P("af", ("grp", "gz"), None, None),
            P("af", None),
        ),
        out_specs=(P("af", ("grp", "gz"), None, None), P("af", "grp")),
        check_vma=False,
    )
```

```python
import math

import jax
import jax.numpy as jnp
from jax import lax
from jax.experimental import pallas as pl
from jax.experimental.pallas import tpu as pltpu
from jax.sharding import PartitionSpec as P

F32 = jnp.float32
BF16 = jnp.bfloat16
VMEM = pl.BlockSpec(memory_space=pltpu.VMEM)
HBM = pl.BlockSpec(memory_space=pltpu.HBM)
PARAMS = pltpu.CompilerParams(vmem_limit_bytes=48 * 1024 * 1024)


def shifted(value, axis, steps):
    count = lax.axis_size(axis)
    leading, last = (max(0, -steps), min(count, count - steps))
    return lax.ppermute(value, axis, [(source, source + steps) for source in range(leading, last)])


def swapped(value, axis, bits):
    count = lax.axis_size(axis)
    return lax.ppermute(value, axis, [(source, source ^ bits) for source in range(count)])


def in_hbm(value):
    return pltpu.with_memory_space_constraint(value, pltpu.HBM)


def halves(value):
    high = value.astype(BF16)
    return high, (value - high.astype(F32)).astype(BF16)


def dot(a, b):
    return lax.dot_general(a, b, (((1,), (0,)), ((), ())), preferred_element_type=F32)


def dot_t(a, b):
    return lax.dot_general(a, b, (((1,), (1,)), ((), ())), preferred_element_type=F32)


def column_taps(cols, out_cols):
    x = lax.broadcasted_iota(jnp.int32, (cols, 3 * out_cols), 0)
    c = lax.broadcasted_iota(jnp.int32, (cols, 3 * out_cols), 1)
    dx = c // out_cols
    return jnp.where(x == 2 * (c - dx * out_cols) + dx - 1, 1.0, 0.0).astype(BF16)


def split_rows(g_ref, filters, out_rows, out_cols, high_ref, low_ref, first=0):
    for q in range(out_rows):
        pair = halves(g_ref[pl.ds(q, filters, stride=out_rows), :])
        for target, half in zip((high_ref, low_ref), pair):
            target[first : first + filters, q * out_cols : (q + 1) * out_cols] = half


def gather_taps(volumes, out_grad):
    filters, _, out_rows, out_cols = out_grad.shape
    channels, planes, rows, cols = volumes[0].shape
    cores = len(volumes)
    count = planes * rows * channels
    width = planes * 9 * cores * channels
    cells = out_rows * out_cols

    def kernel(v_hbm, g_hbm, *refs):
        v_refs = refs[: cores - 1]
        targets, g_targets = refs[cores - 1 : cores + 1], refs[cores + 1 : cores + 3]
        x_refs, d_refs = refs[cores + 3 : cores + 5], refs[cores + 5 : cores + 7]
        own_lanes, lanes, g_ref, sems = refs[cores + 7 :]
        copies = [
            pltpu.make_async_copy(v_hbm.at[:, h * 128 : (h + 1) * 128], own_lanes.at[h], sems.at[h])
            for h in range(cols // 128)
        ] + [pltpu.make_async_copy(g_hbm, g_ref, sems.at[cols // 128])]
        for copy in copies:
            copy.start()
        taps = column_taps(cols, out_cols)
        for core in reversed(range(cores)):
            if core == 0:
                for copy in copies:
                    copy.wait()
            for h in range(cols // 128):
                source = own_lanes.at[h]
                if core:
                    source = lanes
                    lanes[...] = v_refs[core - 1][:, h * 128 : (h + 1) * 128]
                for k in range(planes * rows):
                    pair = halves(source[pl.ds(k, channels, stride=planes * rows), :])
                    for x_ref, half in zip(x_refs, pair):
                        x_ref[k * channels : (k + 1) * channels, h * 128 : (h + 1) * 128] = half
            for x_ref, d_ref, target in zip(x_refs, d_refs, targets):
                d_ref[...] = dot(x_ref[...], taps).astype(BF16)
                for z in range(planes):
                    for dy in range(3):
                        for q in range(out_rows):
                            y = 2 * q + dy - 1
                            for dx in range(3):
                                at = (((z * 3 + dy) * 3 + dx) * cores + core) * channels
                                if y < 0:
                                    piece = jnp.zeros((channels, out_cols), BF16)
                                else:
                                    first = (z * rows + y) * channels
                                    piece = d_ref[first : first + channels, dx * out_cols : (dx + 1) * out_cols]
                                target[at : at + channels, q * out_cols : (q + 1) * out_cols] = piece
        split_rows(g_ref, filters, out_rows, out_cols, *g_targets)

    return pl.pallas_call(
        kernel,
        in_specs=[HBM, HBM] + [VMEM] * (cores - 1),
        out_shape=[jax.ShapeDtypeStruct((width, cells), BF16)] * 2
        + [jax.ShapeDtypeStruct((filters, cells), BF16)] * 2,
        scratch_shapes=[pltpu.VMEM((count, cols), BF16)] * 2
        + [pltpu.VMEM((count, 3 * out_cols), BF16)] * 2
        + [
            pltpu.VMEM((cols // 128, count, 128), F32),
            pltpu.VMEM((count, 128), F32),
            pltpu.VMEM((filters * out_rows, out_cols), F32),
            pltpu.SemaphoreType.DMA((cols // 128 + 1,)),
        ],
        compiler_params=PARAMS,
        name="gather_taps",
    )(in_hbm(volumes[0].reshape(-1, cols)), in_hbm(out_grad.reshape(-1, out_cols)), *[v.reshape(-1, cols) for v in volumes[1:]])


def weight_terms(high, low, own, across):
    filters, _, out_rows, out_cols = across.shape
    cells = out_rows * out_cols

    def kernel(high_ref, low_ref, own_high, own_low, g_ref, out_ref, g_both):
        g_both[:filters, :] = own_high[...]
        g_both[2 * filters : 3 * filters, :] = own_low[...]
        split_rows(g_ref, filters, out_rows, out_cols, g_both.at[filters:], g_both.at[3 * filters :])
        both = dot_t(g_both[...], high_ref[...])
        out_ref[...] = both[: 2 * filters] + both[2 * filters :] + dot_t(g_both[: 2 * filters, :], low_ref[...])

    return pl.pallas_call(
        kernel,
        out_shape=jax.ShapeDtypeStruct((2 * filters, high.shape[0]), F32),
        scratch_shapes=[pltpu.VMEM((4 * filters, cells), BF16)],
        compiler_params=PARAMS,
        name="weight_terms",
    )(high, low, *own, across.reshape(-1, out_cols))


def weight_partial(high, low, terms, above, parts):
    filters, _, out_rows, out_cols = above[0].shape
    cells = out_rows * out_cols
    third = high.shape[0] // 2
    block = filters // parts
    chips = len(above)
    count = chips * filters

    def kernel(high_ref, low_ref, terms_ref, *refs):
        g_refs, out_refs = refs[:chips], refs[chips : chips + parts]
        g_both, total = refs[chips + parts :]
        for j, g_ref in enumerate(g_refs):
            split_rows(g_ref, filters, out_rows, out_cols, g_both.at[:count], g_both.at[count:], j * filters)
        both = dot_t(g_both[...], high_ref[third:, :])
        total[:, :third] = both[:count] + both[count:] + dot_t(g_both[:count, :], low_ref[third:, :])
        total[:, third:] = terms_ref[...]
        slab = lax.axis_index("gz")
        for k in range(parts):
            for j in range(chips):
                first = pl.multiple_of(j * filters + (slab ^ k) * block, 8)
                out_refs[k][j * block : (j + 1) * block, :] = total[pl.ds(first, block), :]

    return pl.pallas_call(
        kernel,
        out_shape=[jax.ShapeDtypeStruct((chips * block, 3 * third), F32)] * parts,
        scratch_shapes=[
            pltpu.VMEM((2 * count, cells), BF16),
            pltpu.VMEM((count, 3 * third), F32),
        ],
        compiler_params=PARAMS,
        name="weight_partial",
    )(high, low, terms, *[g.reshape(-1, out_cols) for g in above])


def add_slabs(pieces, chips):
    rows, width = pieces[0].shape
    block = rows // chips

    def kernel(*refs):
        for j in range(chips):
            value = refs[0][j * block : (j + 1) * block, :]
            for piece in refs[1 : len(pieces)]:
                value = value + piece[j * block : (j + 1) * block, :]
            refs[len(pieces) + j][...] = value

    return pl.pallas_call(
        kernel,
        out_shape=[jax.ShapeDtypeStruct((block, width), F32)] * chips,
        compiler_params=PARAMS,
        name="add_slabs",
    )(*pieces)


def weave_channels(pieces, channels, cores, factor):
    chips = len(pieces)
    block, width = pieces[0].shape
    total = chips * cores * channels
    span = 128
    taps = span // (cores * channels)
    chunks = -(-width // span)

    def kernel(*refs):
        me = lax.axis_index("af")
        row = lax.broadcasted_iota(jnp.int32, (chips * span, taps * total), 0)
        col = lax.broadcasted_iota(jnp.int32, (chips * span, taps * total), 1)
        j = row // span
        inner = row - j * span
        tap = inner // (cores * channels)
        core = (inner // channels) % cores
        owner = me ^ (j * cores + core)
        place = jnp.where(col == tap * total + owner * channels + inner % channels, 1.0, 0.0).astype(BF16)
        for c in range(chunks):
            size = min(span, width - c * span)
            columns = []
            for j in range(chips):
                value = refs[j][:, c * span : c * span + size] * factor
                if size < span:
                    value = jnp.concatenate([value, jnp.zeros((block, span - size), F32)], axis=1)
                columns.append(value)
            wide = jnp.concatenate(columns, axis=1)
            high = wide.astype(BF16).astype(F32)
            rest = wide - high
            middle = rest.astype(BF16).astype(F32)
            stacked = jnp.concatenate([high, middle, rest - middle], axis=0).astype(BF16)
            woven = dot(stacked, place)
            result = woven[:block] + woven[block : 2 * block] + woven[2 * block :]
            first = c * taps * total
            last = min(first + taps * total, 27 * total)
            refs[chips][:, first:last] = result[:, : last - first]

    return pl.pallas_call(
        kernel,
        out_shape=jax.ShapeDtypeStruct((block, 27 * total), F32),
        compiler_params=PARAMS,
        name="weave_channels",
    )(*pieces)


def stack_slabs(pieces):
    block, width = pieces[0].shape
    parts = len(pieces)

    def kernel(*refs):
        slab = lax.axis_index("gz")
        for k in range(parts):
            refs[parts][slab ^ k] = refs[k][...]

    return pl.pallas_call(
        kernel,
        out_shape=jax.ShapeDtypeStruct((parts, block, width), F32),
        compiler_params=PARAMS,
        name="stack_slabs",
    )(*pieces).reshape(parts * block, width)


def pack_weights(weight, cores, channels):
    filters, width = weight.shape
    total = width // 27
    kept = cores * channels
    span = 128 * total // kept
    chunks = -(-width // span)

    def kernel(w_ref, own_ref, other_ref):
        chip = lax.axis_index("af") // cores
        row = lax.broadcasted_iota(jnp.int32, (span, 128), 0)
        col = lax.broadcasted_iota(jnp.int32, (span, 128), 1)
        start = (col // kept) * total + col % kept
        for target, side in ((own_ref, chip), (other_ref, 1 - chip)):
            place = jnp.where(row == start + side * kept, 1.0, 0.0).astype(BF16)
            for c in range(chunks):
                size = min(span, width - c * span)
                value = w_ref[:, c * span : c * span + size]
                if size < span:
                    value = jnp.concatenate([value, jnp.zeros((filters, span - size), F32)], axis=1)
                high = value.astype(BF16).astype(F32)
                rest = value - high
                middle = rest.astype(BF16).astype(F32)
                stacked = jnp.concatenate([high, middle, rest - middle], axis=0).astype(BF16)
                packed = dot(stacked, place)
                result = packed[:filters] + packed[filters : 2 * filters] + packed[2 * filters :]
                last = min(128, 27 * kept - c * 128)
                target[:, c * 128 : c * 128 + last] = result[:, :last]

    return pl.pallas_call(
        kernel,
        out_shape=[jax.ShapeDtypeStruct((filters, 27 * kept), F32)] * 2,
        compiler_params=PARAMS,
        name="pack_weights",
    )(weight)


def input_partial(weights, own, grads, volume_shape, cores):
    channels, planes, rows, cols = volume_shape
    chips = len(weights)
    filters, _, out_rows, out_cols = grads[0].shape
    count = chips * filters
    cells = out_rows * out_cols
    ninth = cores * channels
    padded = -(-27 * ninth // 128) * 128
    third = 9 * ninth

    def kernel(*refs):
        w_refs, own_refs, g_refs = refs[:chips], refs[chips : chips + 2], refs[chips + 2 : 3 * chips + 1]
        out_refs = refs[3 * chips + 1 : 3 * chips + 1 + cores]
        turned, a_both, g_all, t_even, t_odd, woven, lanes = refs[3 * chips + 1 + cores :]
        for first in range(0, padded, 128):
            size = min(128, 27 * ninth - first)
            value = jnp.concatenate([w[:, first : first + size] for w in w_refs], axis=0)
            high = value.astype(BF16).astype(F32)
            value = jnp.concatenate([high, value - high], axis=0)
            if size < 128:
                value = jnp.concatenate([value, jnp.zeros((2 * count, 128 - size), F32)], axis=1)
            turned[first : first + 128, :] = value.T
        core = lax.axis_index("af") % cores
        for tap in range(27):
            for h in range(cores):
                first = pl.multiple_of(tap * ninth + (core ^ h) * channels, 8)
                at = (tap * cores + h) * channels
                a_both[at : at + channels, :] = turned[pl.ds(first, channels), :].astype(BF16)
        for half in range(2):
            g_all[2 * half * count : 2 * half * count + filters, :] = own_refs[half][...]
        for k, g_ref in enumerate(g_refs):
            side, j = (k + 1) // chips, (k + 1) % chips
            first = side * 4 * count
            split_rows(g_ref, filters, out_rows, out_cols, g_all.at[first:], g_all.at[first + 2 * count :], j * filters)
        for at in range(0, 8 * count, 2 * count):
            g_all[at + count : at + 2 * count, :] = g_all[at : at + count, :]
        even = a_both[third : 2 * third, :]
        t_even[...] = dot(jnp.concatenate([even, even], axis=1), g_all[: 4 * count, :])
        odd, above = a_both[2 * third :, :], a_both[:third, :]
        t_odd[...] = dot(jnp.concatenate([odd, odd, above, above], axis=1), g_all[...])
        taps = column_taps(cols, out_cols)
        taps = jnp.concatenate([taps, taps], axis=1)
        for h in reversed(range(cores)):
            for z, terms in enumerate((t_even, t_odd)):
                for y in range(rows):
                    q = y // 2
                    for dx in range(3):

                        def term(dy, at):
                            first = (dy * 3 + dx) * ninth + h * channels
                            return terms[first : first + channels, at * out_cols : (at + 1) * out_cols]

                        if y % 2 == 0:
                            value = term(1, q)
                        else:
                            value = term(2, q)
                            if q + 1 < out_rows:
                                value = value + term(0, q + 1)
                        high, low = halves(value)
                        first = (z * rows + y) * channels
                        woven[first : first + channels, dx * out_cols : (dx + 1) * out_cols] = high
                        woven[first : first + channels, (3 + dx) * out_cols : (4 + dx) * out_cols] = low
            result = dot_t(woven[...], taps)
            for half in range(cols // 128):
                for k in range(planes * rows):
                    piece = result[k * channels : (k + 1) * channels, half * 128 : (half + 1) * 128]
                    lanes[pl.ds(k, channels, stride=planes * rows), :] = piece
                out_refs[h][:, half * 128 : (half + 1) * 128] = lanes[...]

    return pl.pallas_call(
        kernel,
        out_shape=[jax.ShapeDtypeStruct((channels * planes * rows, cols), F32)] * cores,
        scratch_shapes=[
            pltpu.VMEM((padded, 2 * count), F32),
            pltpu.VMEM((27 * ninth, 2 * count), BF16),
            pltpu.VMEM((8 * count, cells), BF16),
            pltpu.VMEM((third, cells), F32),
            pltpu.VMEM((third, cells), F32),
            pltpu.VMEM((planes * rows * channels, 6 * out_cols), BF16),
            pltpu.VMEM((planes * rows * channels, 128), F32),
        ],
        compiler_params=PARAMS,
        name="input_partial",
    )(*weights, *own, *[g.reshape(-1, out_cols) for g in grads])


def below(value, bits):
    parts, groups = lax.axis_size("gz"), lax.axis_size("af")
    pairs = [
        ((slab + 1) * groups + (a ^ bits), slab * groups + a) for slab in range(parts - 1) for a in range(groups)
    ]
    return lax.ppermute(value, ("gz", "af"), pairs)


def fast(volume, out_grad, weight):
    channels, planes, rows, cols = volume.shape
    filters, out_depth, out_rows, out_cols = out_grad.shape
    parts, cores = lax.axis_size("gz"), 2
    factor = 1.0 / math.sqrt(out_depth * parts * out_rows * out_cols)
    across = swapped(out_grad, "af", cores)
    above = [below(out_grad, 0), below(out_grad, cores)]
    mine, theirs = pack_weights(weight, cores, channels)
    weights = [mine, swapped(theirs, "af", cores)]
    high, low, *own = gather_taps([volume, swapped(volume, "af", 1)], out_grad)
    terms = weight_terms(high, low, own, across)
    sent = weight_partial(high, low, terms, above, parts)
    arrived = [sent[0]] + [swapped(sent[k], "gz", k) for k in range(1, parts)]
    inputs = input_partial(weights, own, [across, *above], volume.shape, cores)
    inputs, arrived = lax.optimization_barrier((inputs, arrived))
    input_grad = (inputs[0] + swapped(inputs[1], "af", 1)).reshape(volume.shape)
    sums = add_slabs(arrived, 2)
    woven = weave_channels([sums[0], swapped(sums[1], "af", cores)], channels, cores, factor)
    pieces = [woven] + [swapped(woven, "gz", k) for k in range(1, parts)]
    input_grad, pieces = lax.optimization_barrier((input_grad, pieces))
    weight_grad = stack_slabs(pieces)
    return (input_grad, weight_grad)


def tap_matrix(extended, out_depth, out_rows, out_cols):
    channels = extended.shape[0]
    padded = jnp.pad(extended, ((0, 0), (0, 1), (1, 1), (1, 1)))
    split = padded.reshape(channels, out_depth + 1, 2, out_rows + 1, 2, out_cols + 1, 2)
    pieces = []
    for depth_tap in range(3):
        for row_tap in range(3):
            for col_tap in range(3):
                dz_lo = depth_tap // 2
                dy_lo = row_tap // 2
                dx_lo = col_tap // 2
                pieces.append(
                    split[
                        :,
                        dz_lo : dz_lo + out_depth,
                        depth_tap % 2,
                        dy_lo : dy_lo + out_rows,
                        row_tap % 2,
                        dx_lo : dx_lo + out_cols,
                        col_tap % 2,
                    ]
                )
    stacked = jnp.stack(pieces, axis=0)
    return stacked.reshape(27 * channels, out_depth * out_rows * out_cols)


def place_terms(tap_terms, channels, depth_count, out_rows, out_cols, planes, rows, cols):
    shaped = tap_terms.reshape(27, channels, depth_count, out_rows, out_cols)
    phases = {}
    for depth_tap in range(3):
        for row_tap in range(3):
            for col_tap in range(3):
                index = 9 * depth_tap + 3 * row_tap + col_tap
                dz_lo = depth_tap // 2
                dy_lo = row_tap // 2
                dx_lo = col_tap // 2
                moved = jnp.pad(
                    shaped[index],
                    ((0, 0), (dz_lo, 1 - dz_lo), (dy_lo, 1 - dy_lo), (dx_lo, 1 - dx_lo)),
                )
                parity = (depth_tap % 2, row_tap % 2, col_tap % 2)
                phases[parity] = moved if parity not in phases else phases[parity] + moved
    depth_pairs = []
    for depth_bit in range(2):
        row_pairs = []
        for row_bit in range(2):
            col_pair = jnp.stack(
                [phases[depth_bit, row_bit, 0], phases[depth_bit, row_bit, 1]], axis=-1
            )
            row_pairs.append(col_pair)
        depth_pairs.append(jnp.stack(row_pairs, axis=3))
    woven = jnp.stack(depth_pairs, axis=2)
    canvas = woven.reshape(channels, 2 * (depth_count + 1), 2 * (out_rows + 1), 2 * (out_cols + 1))
    return canvas[:, 1 : planes + 1, 1 : rows + 1, 1 : cols + 1]


def general(volume, out_grad, weight):
    channels, planes, rows, cols = volume.shape
    filters, out_depth, out_rows, out_cols = out_grad.shape
    in_total = weight.shape[1] // 27
    factor = 1.0 / math.sqrt(out_depth * lax.axis_size("gz") * out_rows * out_cols)
    lower_rim = shifted(volume[:, planes - 1 : planes], "gz", 1)
    extended = jnp.concatenate([lower_rim, volume], axis=1)
    upper_rim = shifted(out_grad, "gz", -1)
    grad_ext = jnp.concatenate([out_grad, upper_rim], axis=1)
    grads_all, weight_all = (
        lax.all_gather(grad_ext, "af", axis=0, tiled=True),
        lax.all_gather(weight, "af", axis=0, tiled=True),
    )
    all_filters = grads_all.shape[0]
    channel_first = lax.axis_index("af") * channels
    weight_cube = weight_all.reshape(all_filters, 27, in_total)
    own_weight = lax.dynamic_slice_in_dim(weight_cube, channel_first, channels, 2).reshape(
        all_filters, 27 * channels
    )
    tap_terms = lax.dot_general(
        own_weight,
        grads_all.reshape(all_filters, -1),
        (((0,), (0,)), ((), ())),
        precision=lax.Precision.HIGHEST,
        preferred_element_type=jnp.float32,
    )
    input_grad = place_terms(
        tap_terms, channels, out_depth + 1, out_rows, out_cols, planes, rows, cols
    )
    local_grads = out_grad.reshape(filters, -1)
    portion = lax.all_gather(extended, "af", axis=0, tiled=True)
    count = portion.shape[0]
    tap_rows = tap_matrix(portion, out_depth, out_rows, out_cols)
    partial_grad = lax.dot_general(
        local_grads,
        tap_rows,
        (((1,), (1,)), ((), ())),
        precision=lax.Precision.HIGHEST,
        preferred_element_type=jnp.float32,
    )
    partial_grad = partial_grad.reshape(filters, 27, count)
    summed = lax.psum(partial_grad, "gz")
    weight_grad = (summed * factor).reshape(filters, 27 * in_total)
    return (input_grad, weight_grad)


def local(volume, out_grad, weight):
    channels, planes, rows, _ = volume.shape
    filters, out_depth, out_rows, _ = out_grad.shape
    parts, groups = lax.axis_size("gz"), lax.axis_size("af")
    powers = parts & (parts - 1) == 0 and groups == 4
    whole_tiles = channels == 16 and filters % (8 * parts) == 0 and filters == 32
    if powers and whole_tiles and (planes, out_depth) == (2, 1):
        return fast(volume, out_grad, weight)
    return general(volume, out_grad, weight)


def solution(mesh):
    return jax.shard_map(
        local,
        mesh=mesh,
        in_specs=(
            P("af", ("grp", "gz"), None, None),
            P("af", ("grp", "gz"), None, None),
            P("af", None),
        ),
        out_specs=(P("af", ("grp", "gz"), None, None), P("af", "grp")),
        check_vma=False,
    )
```

```python
import math

import jax
import jax.numpy as jnp
from jax import lax
from jax.experimental import pallas as pl
from jax.experimental.pallas import tpu as pltpu
from jax.sharding import PartitionSpec as P

F32 = jnp.float32
BF16 = jnp.bfloat16
VMEM = pl.BlockSpec(memory_space=pltpu.VMEM)
HBM = pl.BlockSpec(memory_space=pltpu.HBM)
PARAMS = pltpu.CompilerParams(vmem_limit_bytes=48 * 1024 * 1024)


def shifted(value, axis, steps):
    count = lax.axis_size(axis)
    leading, last = (max(0, -steps), min(count, count - steps))
    return lax.ppermute(value, axis, [(source, source + steps) for source in range(leading, last)])


def swapped(value, axis, bits):
    count = lax.axis_size(axis)
    return lax.ppermute(value, axis, [(source, source ^ bits) for source in range(count)])


def in_hbm(value):
    return pltpu.with_memory_space_constraint(value, pltpu.HBM)


def turned_by(value, axis, steps):
    count = lax.axis_size(axis)
    return lax.ppermute(value, axis, [(source, (source + steps) % count) for source in range(count)])


def halves(value):
    high = value.astype(BF16)
    return high, (value - high.astype(F32)).astype(BF16)


def dot(a, b):
    return lax.dot_general(a, b, (((1,), (0,)), ((), ())), preferred_element_type=F32)


def dot_t(a, b):
    return lax.dot_general(a, b, (((1,), (1,)), ((), ())), preferred_element_type=F32)


def column_taps(cols, out_cols):
    x = lax.broadcasted_iota(jnp.int32, (cols, 3 * out_cols), 0)
    c = lax.broadcasted_iota(jnp.int32, (cols, 3 * out_cols), 1)
    dx = c // out_cols
    return jnp.where(x == 2 * (c - dx * out_cols) + dx - 1, 1.0, 0.0).astype(BF16)


def split_rows(g_ref, filters, out_rows, out_cols, high_ref, low_ref, first=0):
    for q in range(out_rows):
        pair = halves(g_ref[pl.ds(q, filters, stride=out_rows), :])
        for target, half in zip((high_ref, low_ref), pair):
            target[first : first + filters, q * out_cols : (q + 1) * out_cols] = half


def pack_columns(w_ref, targets, total, kept, sides):
    filters, width = w_ref.shape
    span = 128 * total // kept
    row = lax.broadcasted_iota(jnp.int32, (span, 128), 0)
    col = lax.broadcasted_iota(jnp.int32, (span, 128), 1)
    start = (col // kept) * total + col % kept
    places = [jnp.where(row == start + side * kept, 1.0, 0.0).astype(BF16) for side in sides]
    for first in range(0, width, span):
        size = min(span, width - first)
        value = w_ref[:, first : first + size]
        if size < span:
            value = jnp.concatenate([value, jnp.zeros((filters, span - size), F32)], axis=1)
        high = value.astype(BF16).astype(F32)
        rest = value - high
        middle = rest.astype(BF16).astype(F32)
        stacked = jnp.concatenate([high, middle, rest - middle], axis=0).astype(BF16)
        at = first * kept // total
        for place, target in zip(places, targets):
            packed = dot(stacked, place)
            result = packed[:filters] + packed[filters : 2 * filters] + packed[2 * filters :]
            last = min(128, 27 * kept - at)
            target[:, at : at + last] = result[:, :last]


def prepare(volumes, out_grad, weight):
    filters, _, out_rows, out_cols = out_grad.shape
    channels, planes, rows, cols = volumes[0].shape
    cores = len(volumes)
    count = planes * rows * channels
    width = planes * 9 * cores * channels
    cells = out_rows * out_cols
    total, kept = weight.shape[1] // 27, cores * channels

    def kernel(v_hbm, g_hbm, w_hbm, *refs):
        v_refs = refs[: cores - 1]
        targets, g_targets = refs[cores - 1 : cores + 1], refs[cores + 1 : cores + 3]
        w_targets = refs[cores + 3 : cores + 5]
        x_refs, d_refs = refs[cores + 5 : cores + 7], refs[cores + 7 : cores + 9]
        own_lanes, lanes, g_ref, w_ref, sems = refs[cores + 9 :]
        copies = [
            pltpu.make_async_copy(v_hbm.at[:, h * 128 : (h + 1) * 128], own_lanes.at[h], sems.at[h])
            for h in range(cols // 128)
        ]
        copies.append(pltpu.make_async_copy(g_hbm, g_ref, sems.at[cols // 128]))
        copies.append(pltpu.make_async_copy(w_hbm, w_ref, sems.at[cols // 128 + 1]))
        for copy in copies:
            copy.start()
        taps = column_taps(cols, out_cols)
        for core in reversed(range(cores)):
            if core == 0:
                for copy in copies:
                    copy.wait()
            for h in range(cols // 128):
                source = own_lanes.at[h]
                if core:
                    source = lanes
                    lanes[...] = v_refs[core - 1][:, h * 128 : (h + 1) * 128]
                for k in range(planes * rows):
                    pair = halves(source[pl.ds(k, channels, stride=planes * rows), :])
                    for x_ref, half in zip(x_refs, pair):
                        x_ref[k * channels : (k + 1) * channels, h * 128 : (h + 1) * 128] = half
            for x_ref, d_ref, target in zip(x_refs, d_refs, targets):
                d_ref[...] = dot(x_ref[...], taps).astype(BF16)
                for z in range(planes):
                    for dy in range(3):
                        for q in range(out_rows):
                            y = 2 * q + dy - 1
                            for dx in range(3):
                                at = (((z * 3 + dy) * 3 + dx) * cores + core) * channels
                                if y < 0:
                                    piece = jnp.zeros((channels, out_cols), BF16)
                                else:
                                    first = (z * rows + y) * channels
                                    piece = d_ref[first : first + channels, dx * out_cols : (dx + 1) * out_cols]
                                target[at : at + channels, q * out_cols : (q + 1) * out_cols] = piece
        split_rows(g_ref, filters, out_rows, out_cols, *g_targets)
        chip = lax.axis_index("af") // cores
        pack_columns(w_ref, w_targets, total, kept, (chip, 1 - chip))

    return pl.pallas_call(
        kernel,
        in_specs=[HBM, HBM, HBM] + [VMEM] * (cores - 1),
        out_shape=[jax.ShapeDtypeStruct((width, cells), BF16)] * 2
        + [jax.ShapeDtypeStruct((filters, cells), BF16)] * 2
        + [jax.ShapeDtypeStruct((filters, 27 * kept), F32)] * 2,
        scratch_shapes=[pltpu.VMEM((count, cols), BF16)] * 2
        + [pltpu.VMEM((count, 3 * out_cols), BF16)] * 2
        + [
            pltpu.VMEM((cols // 128, count, 128), F32),
            pltpu.VMEM((count, 128), F32),
            pltpu.VMEM((filters * out_rows, out_cols), F32),
            pltpu.VMEM(weight.shape, F32),
            pltpu.SemaphoreType.DMA((cols // 128 + 2,)),
        ],
        compiler_params=PARAMS,
        name="prepare",
    )(in_hbm(volumes[0].reshape(-1, cols)), in_hbm(out_grad.reshape(-1, out_cols)), in_hbm(weight), *[v.reshape(-1, cols) for v in volumes[1:]])


def weight_terms(high, low, own, across):
    filters, _, out_rows, out_cols = across.shape
    cells = out_rows * out_cols

    def kernel(high_ref, low_ref, own_high, own_low, g_ref, out_ref, g_both):
        g_both[:filters, :] = own_high[...]
        g_both[2 * filters : 3 * filters, :] = own_low[...]
        split_rows(g_ref, filters, out_rows, out_cols, g_both.at[filters:], g_both.at[3 * filters :])
        both = dot_t(g_both[...], high_ref[...])
        out_ref[...] = both[: 2 * filters] + both[2 * filters :] + dot_t(g_both[: 2 * filters, :], low_ref[...])

    return pl.pallas_call(
        kernel,
        out_shape=jax.ShapeDtypeStruct((2 * filters, high.shape[0]), F32),
        scratch_shapes=[pltpu.VMEM((4 * filters, cells), BF16)],
        compiler_params=PARAMS,
        name="weight_terms",
    )(high, low, *own, across.reshape(-1, out_cols))


def weight_partial(high, low, terms, above, parts):
    filters, _, out_rows, out_cols = above[0].shape
    cells = out_rows * out_cols
    third = high.shape[0] // 2
    block = filters // parts
    chips = len(above)
    count = chips * filters

    def kernel(high_ref, low_ref, terms_ref, *refs):
        g_refs, out_refs = refs[:chips], refs[chips : chips + parts]
        g_both, total = refs[chips + parts :]
        for j, g_ref in enumerate(g_refs):
            split_rows(g_ref, filters, out_rows, out_cols, g_both.at[:count], g_both.at[count:], j * filters)
        both = dot_t(g_both[...], high_ref[third:, :])
        total[:, :third] = both[:count] + both[count:] + dot_t(g_both[:count, :], low_ref[third:, :])
        total[:, third:] = terms_ref[...]
        slab = lax.axis_index("gz")
        for k in range(parts):
            for j in range(chips):
                first = pl.multiple_of(j * filters + lax.rem(slab + k, parts) * block, 8)
                out_refs[k][j * block : (j + 1) * block, :] = total[pl.ds(first, block), :]

    return pl.pallas_call(
        kernel,
        out_shape=[jax.ShapeDtypeStruct((chips * block, 3 * third), F32)] * parts,
        scratch_shapes=[
            pltpu.VMEM((2 * count, cells), BF16),
            pltpu.VMEM((count, 3 * third), F32),
        ],
        compiler_params=PARAMS,
        name="weight_partial",
    )(high, low, terms, *[g.reshape(-1, out_cols) for g in above])


def add_slabs(pieces, chips):
    rows, width = pieces[0].shape
    block = rows // chips

    def kernel(*refs):
        for j in range(chips):
            value = refs[0][j * block : (j + 1) * block, :]
            for piece in refs[1 : len(pieces)]:
                value = value + piece[j * block : (j + 1) * block, :]
            refs[len(pieces) + j][...] = value

    return pl.pallas_call(
        kernel,
        out_shape=[jax.ShapeDtypeStruct((block, width), F32)] * chips,
        compiler_params=PARAMS,
        name="add_slabs",
    )(*pieces)


def channel_places(me, chips, cores, channels):
    total = chips * cores * channels
    taps = 128 // (cores * channels)
    row = lax.broadcasted_iota(jnp.int32, (chips * 128, taps * total), 0)
    col = lax.broadcasted_iota(jnp.int32, (chips * 128, taps * total), 1)
    j = row // 128
    inner = row - j * 128
    tap = inner // (cores * channels)
    owner = me ^ (j * cores + (inner // channels) % cores)
    return jnp.where(col == tap * total + owner * channels + inner % channels, 1.0, 0.0).astype(BF16)


def weave_channels(pieces, place, channels, cores, factor):
    chips = len(pieces)
    block, width = pieces[0].shape
    total = chips * cores * channels
    span = 128
    taps = span // (cores * channels)
    chunks = -(-width // span)

    def kernel(place_ref, *refs):
        place = place_ref[...]
        for c in range(chunks):
            size = min(span, width - c * span)
            columns = []
            for j in range(chips):
                value = refs[j][:, c * span : c * span + size] * factor
                if size < span:
                    value = jnp.concatenate([value, jnp.zeros((block, span - size), F32)], axis=1)
                columns.append(value)
            wide = jnp.concatenate(columns, axis=1)
            high = wide.astype(BF16).astype(F32)
            rest = wide - high
            middle = rest.astype(BF16).astype(F32)
            stacked = jnp.concatenate([high, middle, rest - middle], axis=0).astype(BF16)
            woven = dot(stacked, place)
            result = woven[:block] + woven[block : 2 * block] + woven[2 * block :]
            first = c * taps * total
            last = min(first + taps * total, 27 * total)
            refs[chips][:, first:last] = result[:, : last - first]

    return pl.pallas_call(
        kernel,
        out_shape=jax.ShapeDtypeStruct((block, 27 * total), F32),
        compiler_params=PARAMS,
        name="weave_channels",
    )(place, *pieces)


def stack_slabs(pieces):
    block, width = pieces[0].shape
    parts = len(pieces)

    def kernel(*refs):
        slab = lax.axis_index("gz")
        for k in range(parts):
            refs[parts][lax.rem(slab + parts - k, parts)] = refs[k][...]

    return pl.pallas_call(
        kernel,
        out_shape=jax.ShapeDtypeStruct((parts, block, width), F32),
        compiler_params=PARAMS,
        name="stack_slabs",
    )(*pieces).reshape(parts * block, width)


def input_partial(weights, own, grads, volume_shape, cores):
    channels, planes, rows, cols = volume_shape
    chips = len(weights)
    filters, _, out_rows, out_cols = grads[0].shape
    count = chips * filters
    cells = out_rows * out_cols
    ninth = cores * channels
    padded = -(-27 * ninth // 128) * 128
    third = 9 * ninth

    def kernel(*refs):
        w_refs, own_refs, g_refs = refs[:chips], refs[chips : chips + 2], refs[chips + 2 : 3 * chips + 1]
        out_refs, place_ref = refs[3 * chips + 1 : 3 * chips + 1 + cores], refs[3 * chips + 1 + cores]
        turned, a_both, g_all, t_even, t_odd, woven, lanes = refs[3 * chips + 2 + cores :]
        me = lax.axis_index("af")
        place_ref[...] = channel_places(me, chips, cores, channels)
        for first in range(0, padded, 128):
            size = min(128, 27 * ninth - first)
            value = jnp.concatenate([w[:, first : first + size] for w in w_refs], axis=0)
            high = value.astype(BF16).astype(F32)
            value = jnp.concatenate([high, value - high], axis=0)
            if size < 128:
                value = jnp.concatenate([value, jnp.zeros((2 * count, 128 - size), F32)], axis=1)
            turned[first : first + 128, :] = value.T
        core = me % cores
        for tap in range(27):
            for h in range(cores):
                first = pl.multiple_of(tap * ninth + (core ^ h) * channels, 8)
                at = (tap * cores + h) * channels
                a_both[at : at + channels, :] = turned[pl.ds(first, channels), :].astype(BF16)
        for half in range(2):
            g_all[2 * half * count : 2 * half * count + filters, :] = own_refs[half][...]
        for k, g_ref in enumerate(g_refs):
            side, j = (1, k) if k < chips else (0, k - chips + 1)
            first = side * 4 * count
            split_rows(g_ref, filters, out_rows, out_cols, g_all.at[first:], g_all.at[first + 2 * count :], j * filters)
        for at in range(0, 8 * count, 2 * count):
            g_all[at + count : at + 2 * count, :] = g_all[at : at + count, :]
        even = a_both[third : 2 * third, :]
        t_even[...] = dot(jnp.concatenate([even, even], axis=1), g_all[: 4 * count, :])
        odd, above = a_both[2 * third :, :], a_both[:third, :]
        t_odd[...] = dot(jnp.concatenate([odd, odd, above, above], axis=1), g_all[...])
        taps = column_taps(cols, out_cols)
        taps = jnp.concatenate([taps, taps], axis=1)
        for h in reversed(range(cores)):
            for z, terms in enumerate((t_even, t_odd)):
                for y in range(rows):
                    q = y // 2
                    for dx in range(3):

                        def term(dy, at):
                            first = (dy * 3 + dx) * ninth + h * channels
                            return terms[first : first + channels, at * out_cols : (at + 1) * out_cols]

                        if y % 2 == 0:
                            value = term(1, q)
                        else:
                            value = term(2, q)
                            if q + 1 < out_rows:
                                value = value + term(0, q + 1)
                        high, low = halves(value)
                        first = (z * rows + y) * channels
                        woven[first : first + channels, dx * out_cols : (dx + 1) * out_cols] = high
                        woven[first : first + channels, (3 + dx) * out_cols : (4 + dx) * out_cols] = low
            result = dot_t(woven[...], taps)
            for half in range(cols // 128):
                for k in range(planes * rows):
                    piece = result[k * channels : (k + 1) * channels, half * 128 : (half + 1) * 128]
                    lanes[pl.ds(k, channels, stride=planes * rows), :] = piece
                out_refs[h][:, half * 128 : (half + 1) * 128] = lanes[...]

    return pl.pallas_call(
        kernel,
        out_shape=[jax.ShapeDtypeStruct((channels * planes * rows, cols), F32)] * cores
        + [jax.ShapeDtypeStruct((chips * 128, 128 * chips), BF16)],
        scratch_shapes=[
            pltpu.VMEM((padded, 2 * count), F32),
            pltpu.VMEM((27 * ninth, 2 * count), BF16),
            pltpu.VMEM((8 * count, cells), BF16),
            pltpu.VMEM((third, cells), F32),
            pltpu.VMEM((third, cells), F32),
            pltpu.VMEM((planes * rows * channels, 6 * out_cols), BF16),
            pltpu.VMEM((planes * rows * channels, 128), F32),
        ],
        compiler_params=PARAMS,
        name="input_partial",
    )(*weights, *own, *[g.reshape(-1, out_cols) for g in grads])


def below(value, bits):
    parts, groups = lax.axis_size("gz"), lax.axis_size("af")
    pairs = [
        ((slab + 1) * groups + (a ^ bits), slab * groups + a) for slab in range(parts - 1) for a in range(groups)
    ]
    return lax.ppermute(value, ("gz", "af"), pairs)


def fast(volume, out_grad, weight):
    channels, planes, rows, cols = volume.shape
    filters, out_depth, out_rows, out_cols = out_grad.shape
    parts, cores = lax.axis_size("gz"), 2
    factor = 1.0 / math.sqrt(out_depth * parts * out_rows * out_cols)
    across = swapped(out_grad, "af", cores)
    above = [below(out_grad, 0), below(out_grad, cores)]
    high, low, *own, mine, theirs = prepare([volume, swapped(volume, "af", 1)], out_grad, weight)
    weights = [mine, swapped(theirs, "af", cores)]
    terms = weight_terms(high, low, own, across)
    sent = weight_partial(high, low, terms, above, parts)
    arrived = [sent[0]] + [turned_by(sent[k], "gz", k) for k in (1, 3, 2)]
    *inputs, place = input_partial(weights, own, [*above, across], volume.shape, cores)
    inputs, arrived = lax.optimization_barrier((inputs, arrived))
    input_grad = (inputs[0] + swapped(inputs[1], "af", 1)).reshape(volume.shape)
    sums = add_slabs(arrived, 2)
    woven = weave_channels([sums[0], swapped(sums[1], "af", cores)], place, channels, cores, factor)
    gathered = {k: turned_by(woven, "gz", k) for k in (1, 2, 3)}
    pieces = [woven] + [gathered[k] for k in range(1, parts)]
    input_grad, pieces = lax.optimization_barrier((input_grad, pieces))
    weight_grad = stack_slabs(pieces)
    return (input_grad, weight_grad)


def tap_matrix(extended, out_depth, out_rows, out_cols):
    channels = extended.shape[0]
    padded = jnp.pad(extended, ((0, 0), (0, 1), (1, 1), (1, 1)))
    split = padded.reshape(channels, out_depth + 1, 2, out_rows + 1, 2, out_cols + 1, 2)
    pieces = []
    for depth_tap in range(3):
        for row_tap in range(3):
            for col_tap in range(3):
                dz_lo = depth_tap // 2
                dy_lo = row_tap // 2
                dx_lo = col_tap // 2
                pieces.append(
                    split[
                        :,
                        dz_lo : dz_lo + out_depth,
                        depth_tap % 2,
                        dy_lo : dy_lo + out_rows,
                        row_tap % 2,
                        dx_lo : dx_lo + out_cols,
                        col_tap % 2,
                    ]
                )
    stacked = jnp.stack(pieces, axis=0)
    return stacked.reshape(27 * channels, out_depth * out_rows * out_cols)


def place_terms(tap_terms, channels, depth_count, out_rows, out_cols, planes, rows, cols):
    shaped = tap_terms.reshape(27, channels, depth_count, out_rows, out_cols)
    phases = {}
    for depth_tap in range(3):
        for row_tap in range(3):
            for col_tap in range(3):
                index = 9 * depth_tap + 3 * row_tap + col_tap
                dz_lo = depth_tap // 2
                dy_lo = row_tap // 2
                dx_lo = col_tap // 2
                moved = jnp.pad(
                    shaped[index],
                    ((0, 0), (dz_lo, 1 - dz_lo), (dy_lo, 1 - dy_lo), (dx_lo, 1 - dx_lo)),
                )
                parity = (depth_tap % 2, row_tap % 2, col_tap % 2)
                phases[parity] = moved if parity not in phases else phases[parity] + moved
    depth_pairs = []
    for depth_bit in range(2):
        row_pairs = []
        for row_bit in range(2):
            col_pair = jnp.stack(
                [phases[depth_bit, row_bit, 0], phases[depth_bit, row_bit, 1]], axis=-1
            )
            row_pairs.append(col_pair)
        depth_pairs.append(jnp.stack(row_pairs, axis=3))
    woven = jnp.stack(depth_pairs, axis=2)
    canvas = woven.reshape(channels, 2 * (depth_count + 1), 2 * (out_rows + 1), 2 * (out_cols + 1))
    return canvas[:, 1 : planes + 1, 1 : rows + 1, 1 : cols + 1]


def general(volume, out_grad, weight):
    channels, planes, rows, cols = volume.shape
    filters, out_depth, out_rows, out_cols = out_grad.shape
    in_total = weight.shape[1] // 27
    factor = 1.0 / math.sqrt(out_depth * lax.axis_size("gz") * out_rows * out_cols)
    lower_rim = shifted(volume[:, planes - 1 : planes], "gz", 1)
    extended = jnp.concatenate([lower_rim, volume], axis=1)
    upper_rim = shifted(out_grad, "gz", -1)
    grad_ext = jnp.concatenate([out_grad, upper_rim], axis=1)
    grads_all, weight_all = (
        lax.all_gather(grad_ext, "af", axis=0, tiled=True),
        lax.all_gather(weight, "af", axis=0, tiled=True),
    )
    all_filters = grads_all.shape[0]
    channel_first = lax.axis_index("af") * channels
    weight_cube = weight_all.reshape(all_filters, 27, in_total)
    own_weight = lax.dynamic_slice_in_dim(weight_cube, channel_first, channels, 2).reshape(
        all_filters, 27 * channels
    )
    tap_terms = lax.dot_general(
        own_weight,
        grads_all.reshape(all_filters, -1),
        (((0,), (0,)), ((), ())),
        precision=lax.Precision.HIGHEST,
        preferred_element_type=jnp.float32,
    )
    input_grad = place_terms(
        tap_terms, channels, out_depth + 1, out_rows, out_cols, planes, rows, cols
    )
    local_grads = out_grad.reshape(filters, -1)
    portion = lax.all_gather(extended, "af", axis=0, tiled=True)
    count = portion.shape[0]
    tap_rows = tap_matrix(portion, out_depth, out_rows, out_cols)
    partial_grad = lax.dot_general(
        local_grads,
        tap_rows,
        (((1,), (1,)), ((), ())),
        precision=lax.Precision.HIGHEST,
        preferred_element_type=jnp.float32,
    )
    partial_grad = partial_grad.reshape(filters, 27, count)
    summed = lax.psum(partial_grad, "gz")
    weight_grad = (summed * factor).reshape(filters, 27 * in_total)
    return (input_grad, weight_grad)


def local(volume, out_grad, weight):
    channels, planes, rows, _ = volume.shape
    filters, out_depth, out_rows, _ = out_grad.shape
    parts, groups = lax.axis_size("gz"), lax.axis_size("af")
    powers = parts & (parts - 1) == 0 and groups == 4
    whole_tiles = channels == 16 and filters % (8 * parts) == 0 and filters == 32
    if powers and whole_tiles and (planes, out_depth) == (2, 1):
        return fast(volume, out_grad, weight)
    return general(volume, out_grad, weight)


def solution(mesh):
    return jax.shard_map(
        local,
        mesh=mesh,
        in_specs=(
            P("af", ("grp", "gz"), None, None),
            P("af", ("grp", "gz"), None, None),
            P("af", None),
        ),
        out_specs=(P("af", ("grp", "gz"), None, None), P("af", "grp")),
        check_vma=False,
    )
```

```python
import math

import jax
import jax.numpy as jnp
from jax import lax
from jax.experimental import pallas as pl
from jax.experimental.pallas import tpu as pltpu
from jax.sharding import PartitionSpec as P

F32 = jnp.float32
BF16 = jnp.bfloat16
VMEM = pl.BlockSpec(memory_space=pltpu.VMEM)
HBM = pl.BlockSpec(memory_space=pltpu.HBM)
PARAMS = pltpu.CompilerParams(vmem_limit_bytes=48 * 1024 * 1024)


def shifted(value, axis, steps):
    count = lax.axis_size(axis)
    leading, last = (max(0, -steps), min(count, count - steps))
    return lax.ppermute(value, axis, [(source, source + steps) for source in range(leading, last)])


def swapped(value, axis, bits):
    count = lax.axis_size(axis)
    return lax.ppermute(value, axis, [(source, source ^ bits) for source in range(count)])


def in_hbm(value):
    return pltpu.with_memory_space_constraint(value, pltpu.HBM)


def routes(count, ring, steps):
    place = {slab: at for at, slab in enumerate(ring)}
    return [ring[(place[slab] + steps) % count] for slab in range(count)]


def routed(value, axis, route):
    return lax.ppermute(value, axis, list(enumerate(route)))


def entry(table, index):
    value = table[0]
    for at in range(1, len(table)):
        value = jnp.where(index == at, table[at], value)
    return value


def halves(value):
    high = value.astype(BF16)
    return high, (value - high.astype(F32)).astype(BF16)


def dot(a, b):
    return lax.dot_general(a, b, (((1,), (0,)), ((), ())), preferred_element_type=F32)


def dot_t(a, b):
    return lax.dot_general(a, b, (((1,), (1,)), ((), ())), preferred_element_type=F32)


def column_taps(cols, out_cols):
    x = lax.broadcasted_iota(jnp.int32, (cols, 3 * out_cols), 0)
    c = lax.broadcasted_iota(jnp.int32, (cols, 3 * out_cols), 1)
    dx = c // out_cols
    return jnp.where(x == 2 * (c - dx * out_cols) + dx - 1, 1.0, 0.0).astype(BF16)


def split_rows(g_ref, filters, out_rows, out_cols, high_ref, low_ref, first=0):
    for q in range(out_rows):
        pair = halves(g_ref[pl.ds(q, filters, stride=out_rows), :])
        for target, half in zip((high_ref, low_ref), pair):
            target[first : first + filters, q * out_cols : (q + 1) * out_cols] = half


def pack_columns(w_ref, targets, total, kept, sides):
    filters, width = w_ref.shape
    span = 128 * total // kept
    row = lax.broadcasted_iota(jnp.int32, (span, 128), 0)
    col = lax.broadcasted_iota(jnp.int32, (span, 128), 1)
    start = (col // kept) * total + col % kept
    places = [jnp.where(row == start + side * kept, 1.0, 0.0).astype(BF16) for side in sides]
    for first in range(0, width, span):
        size = min(span, width - first)
        value = w_ref[:, first : first + size]
        if size < span:
            value = jnp.concatenate([value, jnp.zeros((filters, span - size), F32)], axis=1)
        high = value.astype(BF16).astype(F32)
        rest = value - high
        middle = rest.astype(BF16).astype(F32)
        stacked = jnp.concatenate([high, middle, rest - middle], axis=0).astype(BF16)
        at = first * kept // total
        for place, target in zip(places, targets):
            packed = dot(stacked, place)
            result = packed[:filters] + packed[filters : 2 * filters] + packed[2 * filters :]
            last = min(128, 27 * kept - at)
            target[:, at : at + last] = result[:, :last]


def prepare(volumes, out_grad, weight):
    filters, _, out_rows, out_cols = out_grad.shape
    channels, planes, rows, cols = volumes[0].shape
    cores = len(volumes)
    count = planes * rows * channels
    width = planes * 9 * cores * channels
    cells = out_rows * out_cols
    total, kept = weight.shape[1] // 27, cores * channels

    def kernel(v_hbm, g_hbm, w_hbm, *refs):
        v_refs = refs[: cores - 1]
        targets, g_targets = refs[cores - 1 : cores + 1], refs[cores + 1 : cores + 3]
        w_targets = refs[cores + 3 : cores + 5]
        x_refs, d_refs = refs[cores + 5 : cores + 7], refs[cores + 7 : cores + 9]
        own_lanes, lanes, g_ref, w_ref, sems = refs[cores + 9 :]
        copies = [
            pltpu.make_async_copy(v_hbm.at[:, h * 128 : (h + 1) * 128], own_lanes.at[h], sems.at[h])
            for h in range(cols // 128)
        ]
        copies.append(pltpu.make_async_copy(g_hbm, g_ref, sems.at[cols // 128]))
        copies.append(pltpu.make_async_copy(w_hbm, w_ref, sems.at[cols // 128 + 1]))
        for copy in copies:
            copy.start()
        taps = column_taps(cols, out_cols)
        for core in reversed(range(cores)):
            if core == 0:
                for copy in copies:
                    copy.wait()
            for h in range(cols // 128):
                source = own_lanes.at[h]
                if core:
                    source = lanes
                    lanes[...] = v_refs[core - 1][:, h * 128 : (h + 1) * 128]
                for k in range(planes * rows):
                    pair = halves(source[pl.ds(k, channels, stride=planes * rows), :])
                    for x_ref, half in zip(x_refs, pair):
                        x_ref[k * channels : (k + 1) * channels, h * 128 : (h + 1) * 128] = half
            for x_ref, d_ref, target in zip(x_refs, d_refs, targets):
                d_ref[...] = dot(x_ref[...], taps).astype(BF16)
                for z in range(planes):
                    for dy in range(3):
                        for q in range(out_rows):
                            y = 2 * q + dy - 1
                            for dx in range(3):
                                at = (((z * 3 + dy) * 3 + dx) * cores + core) * channels
                                if y < 0:
                                    piece = jnp.zeros((channels, out_cols), BF16)
                                else:
                                    first = (z * rows + y) * channels
                                    piece = d_ref[first : first + channels, dx * out_cols : (dx + 1) * out_cols]
                                target[at : at + channels, q * out_cols : (q + 1) * out_cols] = piece
        split_rows(g_ref, filters, out_rows, out_cols, *g_targets)
        chip = lax.axis_index("af") // cores
        pack_columns(w_ref, w_targets, total, kept, (chip, 1 - chip))

    return pl.pallas_call(
        kernel,
        in_specs=[HBM, HBM, HBM] + [VMEM] * (cores - 1),
        out_shape=[jax.ShapeDtypeStruct((width, cells), BF16)] * 2
        + [jax.ShapeDtypeStruct((filters, cells), BF16)] * 2
        + [jax.ShapeDtypeStruct((filters, 27 * kept), F32)] * 2,
        scratch_shapes=[pltpu.VMEM((count, cols), BF16)] * 2
        + [pltpu.VMEM((count, 3 * out_cols), BF16)] * 2
        + [
            pltpu.VMEM((cols // 128, count, 128), F32),
            pltpu.VMEM((count, 128), F32),
            pltpu.VMEM((filters * out_rows, out_cols), F32),
            pltpu.VMEM(weight.shape, F32),
            pltpu.SemaphoreType.DMA((cols // 128 + 2,)),
        ],
        compiler_params=PARAMS,
        name="prepare",
    )(in_hbm(volumes[0].reshape(-1, cols)), in_hbm(out_grad.reshape(-1, out_cols)), in_hbm(weight), *[v.reshape(-1, cols) for v in volumes[1:]])


def weight_terms(high, low, own, across):
    filters, _, out_rows, out_cols = across.shape
    cells = out_rows * out_cols

    def kernel(high_ref, low_ref, own_high, own_low, g_ref, out_ref, g_both):
        g_both[:filters, :] = own_high[...]
        g_both[2 * filters : 3 * filters, :] = own_low[...]
        split_rows(g_ref, filters, out_rows, out_cols, g_both.at[filters:], g_both.at[3 * filters :])
        both = dot_t(g_both[...], high_ref[...])
        out_ref[...] = both[: 2 * filters] + both[2 * filters :] + dot_t(g_both[: 2 * filters, :], low_ref[...])

    return pl.pallas_call(
        kernel,
        out_shape=jax.ShapeDtypeStruct((2 * filters, high.shape[0]), F32),
        scratch_shapes=[pltpu.VMEM((4 * filters, cells), BF16)],
        compiler_params=PARAMS,
        name="weight_terms",
    )(high, low, *own, across.reshape(-1, out_cols))


def weight_partial(high, low, terms, above, routes_out):
    parts = len(routes_out) + 1
    filters, _, out_rows, out_cols = above[0].shape
    cells = out_rows * out_cols
    third = high.shape[0] // 2
    block = filters // parts
    chips = len(above)
    count = chips * filters

    def kernel(high_ref, low_ref, terms_ref, *refs):
        g_refs, out_refs = refs[:chips], refs[chips : chips + parts]
        g_both, total = refs[chips + parts :]
        for j, g_ref in enumerate(g_refs):
            split_rows(g_ref, filters, out_rows, out_cols, g_both.at[:count], g_both.at[count:], j * filters)
        both = dot_t(g_both[...], high_ref[third:, :])
        total[:, :third] = both[:count] + both[count:] + dot_t(g_both[:count, :], low_ref[third:, :])
        total[:, third:] = terms_ref[...]
        slab = lax.axis_index("gz")
        for k in range(parts):
            target = slab if k == 0 else entry(routes_out[k - 1], slab)
            for j in range(chips):
                first = pl.multiple_of(j * filters + target * block, 8)
                out_refs[k][j * block : (j + 1) * block, :] = total[pl.ds(first, block), :]

    return pl.pallas_call(
        kernel,
        out_shape=[jax.ShapeDtypeStruct((chips * block, 3 * third), F32)] * parts,
        scratch_shapes=[
            pltpu.VMEM((2 * count, cells), BF16),
            pltpu.VMEM((count, 3 * third), F32),
        ],
        compiler_params=PARAMS,
        name="weight_partial",
    )(high, low, terms, *[g.reshape(-1, out_cols) for g in above])


def add_slabs(pieces, chips):
    rows, width = pieces[0].shape
    block = rows // chips

    def kernel(*refs):
        for j in range(chips):
            value = refs[0][j * block : (j + 1) * block, :]
            for piece in refs[1 : len(pieces)]:
                value = value + piece[j * block : (j + 1) * block, :]
            refs[len(pieces) + j][...] = value

    return pl.pallas_call(
        kernel,
        out_shape=[jax.ShapeDtypeStruct((block, width), F32)] * chips,
        compiler_params=PARAMS,
        name="add_slabs",
    )(*pieces)


def channel_places(me, chips, cores, channels):
    total = chips * cores * channels
    taps = 128 // (cores * channels)
    row = lax.broadcasted_iota(jnp.int32, (chips * 128, taps * total), 0)
    col = lax.broadcasted_iota(jnp.int32, (chips * 128, taps * total), 1)
    j = row // 128
    inner = row - j * 128
    tap = inner // (cores * channels)
    owner = me ^ (j * cores + (inner // channels) % cores)
    return jnp.where(col == tap * total + owner * channels + inner % channels, 1.0, 0.0).astype(BF16)


def weave_channels(pieces, place, channels, cores, factor):
    chips = len(pieces)
    block, width = pieces[0].shape
    total = chips * cores * channels
    span = 128
    taps = span // (cores * channels)
    chunks = -(-width // span)

    def kernel(place_ref, *refs):
        place = place_ref[...]
        for c in range(chunks):
            size = min(span, width - c * span)
            columns = []
            for j in range(chips):
                value = refs[j][:, c * span : c * span + size] * factor
                if size < span:
                    value = jnp.concatenate([value, jnp.zeros((block, span - size), F32)], axis=1)
                columns.append(value)
            wide = jnp.concatenate(columns, axis=1)
            high = wide.astype(BF16).astype(F32)
            rest = wide - high
            middle = rest.astype(BF16).astype(F32)
            stacked = jnp.concatenate([high, middle, rest - middle], axis=0).astype(BF16)
            woven = dot(stacked, place)
            result = woven[:block] + woven[block : 2 * block] + woven[2 * block :]
            first = c * taps * total
            last = min(first + taps * total, 27 * total)
            refs[chips][:, first:last] = result[:, : last - first]

    return pl.pallas_call(
        kernel,
        out_shape=jax.ShapeDtypeStruct((block, 27 * total), F32),
        compiler_params=PARAMS,
        name="weave_channels",
    )(place, *pieces)


def stack_slabs(pieces, back_routes):
    block, width = pieces[0].shape
    parts = len(pieces)

    def kernel(*refs):
        slab = lax.axis_index("gz")
        for k in range(parts):
            source = slab if k == 0 else entry([back_routes[k - 1].index(at) for at in range(parts)], slab)
            refs[parts][source] = refs[k][...]

    return pl.pallas_call(
        kernel,
        out_shape=jax.ShapeDtypeStruct((parts, block, width), F32),
        compiler_params=PARAMS,
        name="stack_slabs",
    )(*pieces).reshape(parts * block, width)


def input_partial(weights, own, grads, volume_shape, cores):
    channels, planes, rows, cols = volume_shape
    chips = len(weights)
    filters, _, out_rows, out_cols = grads[0].shape
    count = chips * filters
    cells = out_rows * out_cols
    ninth = cores * channels
    padded = -(-27 * ninth // 128) * 128
    third = 9 * ninth

    def kernel(*refs):
        w_refs, own_refs, g_refs = refs[:chips], refs[chips : chips + 2], refs[chips + 2 : 3 * chips + 1]
        out_refs, place_ref = refs[3 * chips + 1 : 3 * chips + 1 + cores], refs[3 * chips + 1 + cores]
        turned, a_both, g_all, t_even, t_odd, woven, lanes = refs[3 * chips + 2 + cores :]
        me = lax.axis_index("af")
        place_ref[...] = channel_places(me, chips, cores, channels)
        for first in range(0, padded, 128):
            size = min(128, 27 * ninth - first)
            value = jnp.concatenate([w[:, first : first + size] for w in w_refs], axis=0)
            high = value.astype(BF16).astype(F32)
            value = jnp.concatenate([high, value - high], axis=0)
            if size < 128:
                value = jnp.concatenate([value, jnp.zeros((2 * count, 128 - size), F32)], axis=1)
            turned[first : first + 128, :] = value.T
        core = me % cores
        for tap in range(27):
            for h in range(cores):
                first = pl.multiple_of(tap * ninth + (core ^ h) * channels, 8)
                at = (tap * cores + h) * channels
                a_both[at : at + channels, :] = turned[pl.ds(first, channels), :].astype(BF16)
        for half in range(2):
            g_all[2 * half * count : 2 * half * count + filters, :] = own_refs[half][...]
        for k, g_ref in enumerate(g_refs):
            side, j = (1, k) if k < chips else (0, k - chips + 1)
            first = side * 4 * count
            split_rows(g_ref, filters, out_rows, out_cols, g_all.at[first:], g_all.at[first + 2 * count :], j * filters)
        for at in range(0, 8 * count, 2 * count):
            g_all[at + count : at + 2 * count, :] = g_all[at : at + count, :]
        even = a_both[third : 2 * third, :]
        t_even[...] = dot(jnp.concatenate([even, even], axis=1), g_all[: 4 * count, :])
        odd, above = a_both[2 * third :, :], a_both[:third, :]
        t_odd[...] = dot(jnp.concatenate([odd, odd, above, above], axis=1), g_all[...])
        taps = column_taps(cols, out_cols)
        taps = jnp.concatenate([taps, taps], axis=1)
        for h in reversed(range(cores)):
            for z, terms in enumerate((t_even, t_odd)):
                for y in range(rows):
                    q = y // 2
                    for dx in range(3):

                        def term(dy, at):
                            first = (dy * 3 + dx) * ninth + h * channels
                            return terms[first : first + channels, at * out_cols : (at + 1) * out_cols]

                        if y % 2 == 0:
                            value = term(1, q)
                        else:
                            value = term(2, q)
                            if q + 1 < out_rows:
                                value = value + term(0, q + 1)
                        high, low = halves(value)
                        first = (z * rows + y) * channels
                        woven[first : first + channels, dx * out_cols : (dx + 1) * out_cols] = high
                        woven[first : first + channels, (3 + dx) * out_cols : (4 + dx) * out_cols] = low
            result = dot_t(woven[...], taps)
            for half in range(cols // 128):
                for k in range(planes * rows):
                    piece = result[k * channels : (k + 1) * channels, half * 128 : (half + 1) * 128]
                    lanes[pl.ds(k, channels, stride=planes * rows), :] = piece
                out_refs[h][:, half * 128 : (half + 1) * 128] = lanes[...]

    return pl.pallas_call(
        kernel,
        out_shape=[jax.ShapeDtypeStruct((channels * planes * rows, cols), F32)] * cores
        + [jax.ShapeDtypeStruct((chips * 128, 128 * chips), BF16)],
        scratch_shapes=[
            pltpu.VMEM((padded, 2 * count), F32),
            pltpu.VMEM((27 * ninth, 2 * count), BF16),
            pltpu.VMEM((8 * count, cells), BF16),
            pltpu.VMEM((third, cells), F32),
            pltpu.VMEM((third, cells), F32),
            pltpu.VMEM((planes * rows * channels, 6 * out_cols), BF16),
            pltpu.VMEM((planes * rows * channels, 128), F32),
        ],
        compiler_params=PARAMS,
        name="input_partial",
    )(*weights, *own, *[g.reshape(-1, out_cols) for g in grads])


def below(value, bits):
    parts, groups = lax.axis_size("gz"), lax.axis_size("af")
    pairs = [
        ((slab + 1) * groups + (a ^ bits), slab * groups + a) for slab in range(parts - 1) for a in range(groups)
    ]
    return lax.ppermute(value, ("gz", "af"), pairs)


def fast(volume, out_grad, weight):
    channels, planes, rows, cols = volume.shape
    filters, out_depth, out_rows, out_cols = out_grad.shape
    parts, cores = lax.axis_size("gz"), 2
    out_routes = [routes(parts, [place ^ (place >> 1) for place in range(parts)], k) for k in range(1, parts)]
    back_routes = [routes(parts, range(parts), k) for k in range(1, parts)]
    factor = 1.0 / math.sqrt(out_depth * parts * out_rows * out_cols)
    across = swapped(out_grad, "af", cores)
    above = [below(out_grad, 0), below(out_grad, cores)]
    high, low, *own, mine, theirs = prepare([volume, swapped(volume, "af", 1)], out_grad, weight)
    weights = [mine, swapped(theirs, "af", cores)]
    terms = weight_terms(high, low, own, across)
    sent = weight_partial(high, low, terms, above, out_routes)
    arrived = [sent[0]] + [routed(piece, "gz", route) for piece, route in zip(sent[1:], out_routes)]
    *inputs, place = input_partial(weights, own, [*above, across], volume.shape, cores)
    inputs, arrived = lax.optimization_barrier((inputs, arrived))
    input_grad = (inputs[0] + swapped(inputs[1], "af", 1)).reshape(volume.shape)
    sums = add_slabs(arrived, 2)
    woven = weave_channels([sums[0], swapped(sums[1], "af", cores)], place, channels, cores, factor)
    pieces = [woven] + [routed(woven, "gz", route) for route in back_routes]
    input_grad, pieces = lax.optimization_barrier((input_grad, pieces))
    weight_grad = stack_slabs(pieces, back_routes)
    return (input_grad, weight_grad)


def tap_matrix(extended, out_depth, out_rows, out_cols):
    channels = extended.shape[0]
    padded = jnp.pad(extended, ((0, 0), (0, 1), (1, 1), (1, 1)))
    split = padded.reshape(channels, out_depth + 1, 2, out_rows + 1, 2, out_cols + 1, 2)
    pieces = []
    for depth_tap in range(3):
        for row_tap in range(3):
            for col_tap in range(3):
                dz_lo = depth_tap // 2
                dy_lo = row_tap // 2
                dx_lo = col_tap // 2
                pieces.append(
                    split[
                        :,
                        dz_lo : dz_lo + out_depth,
                        depth_tap % 2,
                        dy_lo : dy_lo + out_rows,
                        row_tap % 2,
                        dx_lo : dx_lo + out_cols,
                        col_tap % 2,
                    ]
                )
    stacked = jnp.stack(pieces, axis=0)
    return stacked.reshape(27 * channels, out_depth * out_rows * out_cols)


def place_terms(tap_terms, channels, depth_count, out_rows, out_cols, planes, rows, cols):
    shaped = tap_terms.reshape(27, channels, depth_count, out_rows, out_cols)
    phases = {}
    for depth_tap in range(3):
        for row_tap in range(3):
            for col_tap in range(3):
                index = 9 * depth_tap + 3 * row_tap + col_tap
                dz_lo = depth_tap // 2
                dy_lo = row_tap // 2
                dx_lo = col_tap // 2
                moved = jnp.pad(
                    shaped[index],
                    ((0, 0), (dz_lo, 1 - dz_lo), (dy_lo, 1 - dy_lo), (dx_lo, 1 - dx_lo)),
                )
                parity = (depth_tap % 2, row_tap % 2, col_tap % 2)
                phases[parity] = moved if parity not in phases else phases[parity] + moved
    depth_pairs = []
    for depth_bit in range(2):
        row_pairs = []
        for row_bit in range(2):
            col_pair = jnp.stack(
                [phases[depth_bit, row_bit, 0], phases[depth_bit, row_bit, 1]], axis=-1
            )
            row_pairs.append(col_pair)
        depth_pairs.append(jnp.stack(row_pairs, axis=3))
    woven = jnp.stack(depth_pairs, axis=2)
    canvas = woven.reshape(channels, 2 * (depth_count + 1), 2 * (out_rows + 1), 2 * (out_cols + 1))
    return canvas[:, 1 : planes + 1, 1 : rows + 1, 1 : cols + 1]


def general(volume, out_grad, weight):
    channels, planes, rows, cols = volume.shape
    filters, out_depth, out_rows, out_cols = out_grad.shape
    in_total = weight.shape[1] // 27
    factor = 1.0 / math.sqrt(out_depth * lax.axis_size("gz") * out_rows * out_cols)
    lower_rim = shifted(volume[:, planes - 1 : planes], "gz", 1)
    extended = jnp.concatenate([lower_rim, volume], axis=1)
    upper_rim = shifted(out_grad, "gz", -1)
    grad_ext = jnp.concatenate([out_grad, upper_rim], axis=1)
    grads_all, weight_all = (
        lax.all_gather(grad_ext, "af", axis=0, tiled=True),
        lax.all_gather(weight, "af", axis=0, tiled=True),
    )
    all_filters = grads_all.shape[0]
    channel_first = lax.axis_index("af") * channels
    weight_cube = weight_all.reshape(all_filters, 27, in_total)
    own_weight = lax.dynamic_slice_in_dim(weight_cube, channel_first, channels, 2).reshape(
        all_filters, 27 * channels
    )
    tap_terms = lax.dot_general(
        own_weight,
        grads_all.reshape(all_filters, -1),
        (((0,), (0,)), ((), ())),
        precision=lax.Precision.HIGHEST,
        preferred_element_type=jnp.float32,
    )
    input_grad = place_terms(
        tap_terms, channels, out_depth + 1, out_rows, out_cols, planes, rows, cols
    )
    local_grads = out_grad.reshape(filters, -1)
    portion = lax.all_gather(extended, "af", axis=0, tiled=True)
    count = portion.shape[0]
    tap_rows = tap_matrix(portion, out_depth, out_rows, out_cols)
    partial_grad = lax.dot_general(
        local_grads,
        tap_rows,
        (((1,), (1,)), ((), ())),
        precision=lax.Precision.HIGHEST,
        preferred_element_type=jnp.float32,
    )
    partial_grad = partial_grad.reshape(filters, 27, count)
    summed = lax.psum(partial_grad, "gz")
    weight_grad = (summed * factor).reshape(filters, 27 * in_total)
    return (input_grad, weight_grad)


def local(volume, out_grad, weight):
    channels, planes, rows, _ = volume.shape
    filters, out_depth, out_rows, _ = out_grad.shape
    parts, groups = lax.axis_size("gz"), lax.axis_size("af")
    powers = parts & (parts - 1) == 0 and groups == 4
    whole_tiles = channels == 16 and filters % (8 * parts) == 0 and filters == 32
    if powers and whole_tiles and (planes, out_depth) == (2, 1):
        return fast(volume, out_grad, weight)
    return general(volume, out_grad, weight)


def solution(mesh):
    return jax.shard_map(
        local,
        mesh=mesh,
        in_specs=(
            P("af", ("grp", "gz"), None, None),
            P("af", ("grp", "gz"), None, None),
            P("af", None),
        ),
        out_specs=(P("af", ("grp", "gz"), None, None), P("af", "grp")),
        check_vma=False,
    )
```

```python
import math

import jax
import jax.numpy as jnp
from jax import lax
from jax.experimental import pallas as pl
from jax.experimental.pallas import tpu as pltpu
from jax.sharding import PartitionSpec as P

F32 = jnp.float32
BF16 = jnp.bfloat16
VMEM = pl.BlockSpec(memory_space=pltpu.VMEM)
HBM = pl.BlockSpec(memory_space=pltpu.HBM)
COVER = 8000000000
PARAMS = pltpu.CompilerParams(vmem_limit_bytes=48 * 1024 * 1024)


def shifted(value, axis, steps):
    count = lax.axis_size(axis)
    leading, last = (max(0, -steps), min(count, count - steps))
    return lax.ppermute(value, axis, [(source, source + steps) for source in range(leading, last)])


def swapped(value, axis, bits):
    count = lax.axis_size(axis)
    return lax.ppermute(value, axis, [(source, source ^ bits) for source in range(count)])


def in_hbm(value):
    return pltpu.with_memory_space_constraint(value, pltpu.HBM)


def routes(count, ring, steps):
    place = {slab: at for at, slab in enumerate(ring)}
    return [ring[(place[slab] + steps) % count] for slab in range(count)]


def routed(value, axis, route):
    return lax.ppermute(value, axis, list(enumerate(route)))


def entry(table, index):
    value = table[0]
    for at in range(1, len(table)):
        value = jnp.where(index == at, table[at], value)
    return value


def halves(value):
    high = value.astype(BF16)
    return high, (value - high.astype(F32)).astype(BF16)


def dot(a, b):
    return lax.dot_general(a, b, (((1,), (0,)), ((), ())), preferred_element_type=F32)


def dot_t(a, b):
    return lax.dot_general(a, b, (((1,), (1,)), ((), ())), preferred_element_type=F32)


def column_taps(cols, out_cols):
    x = lax.broadcasted_iota(jnp.int32, (cols, 3 * out_cols), 0)
    c = lax.broadcasted_iota(jnp.int32, (cols, 3 * out_cols), 1)
    dx = c // out_cols
    return jnp.where(x == 2 * (c - dx * out_cols) + dx - 1, 1.0, 0.0).astype(BF16)


def split_rows(g_ref, filters, out_rows, out_cols, high_ref, low_ref, first=0):
    for q in range(out_rows):
        pair = halves(g_ref[pl.ds(q, filters, stride=out_rows), :])
        for target, half in zip((high_ref, low_ref), pair):
            target[first : first + filters, q * out_cols : (q + 1) * out_cols] = half


def pack_columns(w_ref, targets, total, kept, sides):
    filters, width = w_ref.shape
    span = 128 * total // kept
    row = lax.broadcasted_iota(jnp.int32, (span, 128), 0)
    col = lax.broadcasted_iota(jnp.int32, (span, 128), 1)
    start = (col // kept) * total + col % kept
    places = [jnp.where(row == start + side * kept, 1.0, 0.0).astype(BF16) for side in sides]
    for first in range(0, width, span):
        size = min(span, width - first)
        value = w_ref[:, first : first + size]
        if size < span:
            value = jnp.concatenate([value, jnp.zeros((filters, span - size), F32)], axis=1)
        high = value.astype(BF16).astype(F32)
        rest = value - high
        middle = rest.astype(BF16).astype(F32)
        stacked = jnp.concatenate([high, middle, rest - middle], axis=0).astype(BF16)
        at = first * kept // total
        for place, target in zip(places, targets):
            packed = dot(stacked, place)
            result = packed[:filters] + packed[filters : 2 * filters] + packed[2 * filters :]
            last = min(128, 27 * kept - at)
            target[:, at : at + last] = result[:, :last]


def prepare(volumes, out_grad, weight):
    filters, _, out_rows, out_cols = out_grad.shape
    channels, planes, rows, cols = volumes[0].shape
    cores = len(volumes)
    count = planes * rows * channels
    width = planes * 9 * cores * channels
    cells = out_rows * out_cols
    total, kept = weight.shape[1] // 27, cores * channels

    def kernel(v_hbm, g_hbm, w_hbm, *refs):
        v_refs = refs[: cores - 1]
        targets, g_targets = refs[cores - 1 : cores + 1], refs[cores + 1 : cores + 3]
        w_targets = refs[cores + 3 : cores + 5]
        x_refs, d_refs = refs[cores + 5 : cores + 7], refs[cores + 7 : cores + 9]
        own_lanes, lanes, g_ref, w_ref, sems = refs[cores + 9 :]
        copies = [
            pltpu.make_async_copy(v_hbm.at[:, h * 128 : (h + 1) * 128], own_lanes.at[h], sems.at[h])
            for h in range(cols // 128)
        ]
        copies.append(pltpu.make_async_copy(g_hbm, g_ref, sems.at[cols // 128]))
        copies.append(pltpu.make_async_copy(w_hbm, w_ref, sems.at[cols // 128 + 1]))
        for copy in copies:
            copy.start()
        taps = column_taps(cols, out_cols)
        for core in reversed(range(cores)):
            if core == 0:
                for copy in copies:
                    copy.wait()
            for h in range(cols // 128):
                source = own_lanes.at[h]
                if core:
                    source = lanes
                    lanes[...] = v_refs[core - 1][:, h * 128 : (h + 1) * 128]
                for k in range(planes * rows):
                    pair = halves(source[pl.ds(k, channels, stride=planes * rows), :])
                    for x_ref, half in zip(x_refs, pair):
                        x_ref[k * channels : (k + 1) * channels, h * 128 : (h + 1) * 128] = half
            for x_ref, d_ref, target in zip(x_refs, d_refs, targets):
                d_ref[...] = dot(x_ref[...], taps).astype(BF16)
                for z in range(planes):
                    for dy in range(3):
                        for q in range(out_rows):
                            y = 2 * q + dy - 1
                            for dx in range(3):
                                at = (((z * 3 + dy) * 3 + dx) * cores + core) * channels
                                if y < 0:
                                    piece = jnp.zeros((channels, out_cols), BF16)
                                else:
                                    first = (z * rows + y) * channels
                                    piece = d_ref[first : first + channels, dx * out_cols : (dx + 1) * out_cols]
                                target[at : at + channels, q * out_cols : (q + 1) * out_cols] = piece
        split_rows(g_ref, filters, out_rows, out_cols, *g_targets)
        chip = lax.axis_index("af") // cores
        pack_columns(w_ref, w_targets, total, kept, (chip, 1 - chip))

    return pl.pallas_call(
        kernel,
        in_specs=[HBM, HBM, HBM] + [VMEM] * (cores - 1),
        out_shape=[jax.ShapeDtypeStruct((width, cells), BF16)] * 2
        + [jax.ShapeDtypeStruct((filters, cells), BF16)] * 2
        + [jax.ShapeDtypeStruct((filters, 27 * kept), F32)] * 2,
        scratch_shapes=[pltpu.VMEM((count, cols), BF16)] * 2
        + [pltpu.VMEM((count, 3 * out_cols), BF16)] * 2
        + [
            pltpu.VMEM((cols // 128, count, 128), F32),
            pltpu.VMEM((count, 128), F32),
            pltpu.VMEM((filters * out_rows, out_cols), F32),
            pltpu.VMEM(weight.shape, F32),
            pltpu.SemaphoreType.DMA((cols // 128 + 2,)),
        ],
        compiler_params=PARAMS,
        name="prepare",
    )(in_hbm(volumes[0].reshape(-1, cols)), in_hbm(out_grad.reshape(-1, out_cols)), in_hbm(weight), *[v.reshape(-1, cols) for v in volumes[1:]])


def weight_terms(high, low, own, across):
    filters, _, out_rows, out_cols = across.shape
    cells = out_rows * out_cols

    def kernel(high_ref, low_ref, own_high, own_low, g_ref, out_ref, g_both):
        g_both[:filters, :] = own_high[...]
        g_both[2 * filters : 3 * filters, :] = own_low[...]
        split_rows(g_ref, filters, out_rows, out_cols, g_both.at[filters:], g_both.at[3 * filters :])
        both = dot_t(g_both[...], high_ref[...])
        out_ref[...] = both[: 2 * filters] + both[2 * filters :] + dot_t(g_both[: 2 * filters, :], low_ref[...])

    return pl.pallas_call(
        kernel,
        out_shape=jax.ShapeDtypeStruct((2 * filters, high.shape[0]), F32),
        scratch_shapes=[pltpu.VMEM((4 * filters, cells), BF16)],
        compiler_params=PARAMS,
        name="weight_terms",
    )(high, low, *own, across.reshape(-1, out_cols))


def weight_partial(high, low, terms, above, routes_out):
    parts = len(routes_out) + 1
    filters, _, out_rows, out_cols = above[0].shape
    cells = out_rows * out_cols
    third = high.shape[0] // 2
    block = filters // parts
    chips = len(above)
    count = chips * filters

    def kernel(high_ref, low_ref, terms_ref, *refs):
        g_refs, out_refs = refs[:chips], refs[chips : chips + parts]
        g_both, total = refs[chips + parts :]
        for j, g_ref in enumerate(g_refs):
            split_rows(g_ref, filters, out_rows, out_cols, g_both.at[:count], g_both.at[count:], j * filters)
        both = dot_t(g_both[...], high_ref[third:, :])
        total[:, :third] = both[:count] + both[count:] + dot_t(g_both[:count, :], low_ref[third:, :])
        total[:, third:] = terms_ref[...]
        slab = lax.axis_index("gz")
        for k in range(parts):
            target = slab if k == 0 else entry(routes_out[k - 1], slab)
            for j in range(chips):
                first = pl.multiple_of(j * filters + target * block, 8)
                out_refs[k][j * block : (j + 1) * block, :] = total[pl.ds(first, block), :]

    return pl.pallas_call(
        kernel,
        out_shape=[jax.ShapeDtypeStruct((chips * block, 3 * third), F32)] * parts,
        scratch_shapes=[
            pltpu.VMEM((2 * count, cells), BF16),
            pltpu.VMEM((count, 3 * third), F32),
        ],
        compiler_params=PARAMS,
        name="weight_partial",
    )(high, low, terms, *[g.reshape(-1, out_cols) for g in above])


def add_slabs(pieces, chips, after):
    rows, width = pieces[0].shape
    block = rows // chips

    def kernel(after_ref, *refs):
        for j in range(chips):
            value = refs[0][j * block : (j + 1) * block, :]
            for piece in refs[1 : len(pieces)]:
                value = value + piece[j * block : (j + 1) * block, :]
            refs[len(pieces) + j][...] = value

    return pl.pallas_call(
        kernel,
        in_specs=[pl.BlockSpec(memory_space=pl.ANY)] + [VMEM] * len(pieces),
        out_shape=[jax.ShapeDtypeStruct((block, width), F32)] * chips,
        compiler_params=PARAMS,
        name="add_slabs",
    )(after, *pieces)


def channel_places(me, chips, cores, channels):
    total = chips * cores * channels
    taps = 128 // (cores * channels)
    row = lax.broadcasted_iota(jnp.int32, (chips * 128, taps * total), 0)
    col = lax.broadcasted_iota(jnp.int32, (chips * 128, taps * total), 1)
    j = row // 128
    inner = row - j * 128
    tap = inner // (cores * channels)
    owner = me ^ (j * cores + (inner // channels) % cores)
    return jnp.where(col == tap * total + owner * channels + inner % channels, 1.0, 0.0).astype(BF16)


def weave_channels(pieces, place, channels, cores, factor):
    chips = len(pieces)
    block, width = pieces[0].shape
    total = chips * cores * channels
    span = 128
    taps = span // (cores * channels)
    chunks = -(-width // span)

    def kernel(place_ref, *refs):
        place = place_ref[...]
        for c in range(chunks):
            size = min(span, width - c * span)
            columns = []
            for j in range(chips):
                value = refs[j][:, c * span : c * span + size] * factor
                if size < span:
                    value = jnp.concatenate([value, jnp.zeros((block, span - size), F32)], axis=1)
                columns.append(value)
            wide = jnp.concatenate(columns, axis=1)
            high = wide.astype(BF16).astype(F32)
            rest = wide - high
            middle = rest.astype(BF16).astype(F32)
            stacked = jnp.concatenate([high, middle, rest - middle], axis=0).astype(BF16)
            woven = dot(stacked, place)
            result = woven[:block] + woven[block : 2 * block] + woven[2 * block :]
            first = c * taps * total
            last = min(first + taps * total, 27 * total)
            refs[chips][:, first:last] = result[:, : last - first]

    return pl.pallas_call(
        kernel,
        out_shape=jax.ShapeDtypeStruct((block, 27 * total), F32),
        cost_estimate=pl.CostEstimate(flops=COVER, bytes_accessed=8000000, transcendentals=0),
        compiler_params=PARAMS,
        name="weave_channels",
    )(place, *pieces)


def stack_slabs(pieces, back_routes):
    block, width = pieces[0].shape
    parts = len(pieces)

    def kernel(*refs):
        slab = lax.axis_index("gz")
        for k in range(parts):
            source = slab if k == 0 else entry([back_routes[k - 1].index(at) for at in range(parts)], slab)
            refs[parts][source] = refs[k][...]

    return pl.pallas_call(
        kernel,
        out_shape=jax.ShapeDtypeStruct((parts, block, width), F32),
        compiler_params=PARAMS,
        name="stack_slabs",
    )(*pieces).reshape(parts * block, width)


def input_partial(weights, own, grads, volume_shape, cores):
    channels, planes, rows, cols = volume_shape
    chips = len(weights)
    filters, _, out_rows, out_cols = grads[0].shape
    count = chips * filters
    cells = out_rows * out_cols
    ninth = cores * channels
    padded = -(-27 * ninth // 128) * 128
    third = 9 * ninth

    def kernel(*refs):
        w_refs, own_refs, g_refs = refs[:chips], refs[chips : chips + 2], refs[chips + 2 : 3 * chips + 1]
        out_refs, place_ref = refs[3 * chips + 1 : 3 * chips + 1 + cores], refs[3 * chips + 1 + cores]
        turned, a_both, g_all, t_even, t_odd, woven, lanes = refs[3 * chips + 2 + cores :]
        me = lax.axis_index("af")
        place_ref[...] = channel_places(me, chips, cores, channels)
        for first in range(0, padded, 128):
            size = min(128, 27 * ninth - first)
            value = jnp.concatenate([w[:, first : first + size] for w in w_refs], axis=0)
            high = value.astype(BF16).astype(F32)
            value = jnp.concatenate([high, value - high], axis=0)
            if size < 128:
                value = jnp.concatenate([value, jnp.zeros((2 * count, 128 - size), F32)], axis=1)
            turned[first : first + 128, :] = value.T
        core = me % cores
        for tap in range(27):
            for h in range(cores):
                first = pl.multiple_of(tap * ninth + (core ^ h) * channels, 8)
                at = (tap * cores + h) * channels
                a_both[at : at + channels, :] = turned[pl.ds(first, channels), :].astype(BF16)
        for half in range(2):
            g_all[2 * half * count : 2 * half * count + filters, :] = own_refs[half][...]
        for k, g_ref in enumerate(g_refs):
            side, j = (1, k) if k < chips else (0, k - chips + 1)
            first = side * 4 * count
            split_rows(g_ref, filters, out_rows, out_cols, g_all.at[first:], g_all.at[first + 2 * count :], j * filters)
        for at in range(0, 8 * count, 2 * count):
            g_all[at + count : at + 2 * count, :] = g_all[at : at + count, :]
        even = a_both[third : 2 * third, :]
        t_even[...] = dot(jnp.concatenate([even, even], axis=1), g_all[: 4 * count, :])
        odd, above = a_both[2 * third :, :], a_both[:third, :]
        t_odd[...] = dot(jnp.concatenate([odd, odd, above, above], axis=1), g_all[...])
        taps = column_taps(cols, out_cols)
        taps = jnp.concatenate([taps, taps], axis=1)
        for h in reversed(range(cores)):
            for z, terms in enumerate((t_even, t_odd)):
                for y in range(rows):
                    q = y // 2
                    for dx in range(3):

                        def term(dy, at):
                            first = (dy * 3 + dx) * ninth + h * channels
                            return terms[first : first + channels, at * out_cols : (at + 1) * out_cols]

                        if y % 2 == 0:
                            value = term(1, q)
                        else:
                            value = term(2, q)
                            if q + 1 < out_rows:
                                value = value + term(0, q + 1)
                        high, low = halves(value)
                        first = (z * rows + y) * channels
                        woven[first : first + channels, dx * out_cols : (dx + 1) * out_cols] = high
                        woven[first : first + channels, (3 + dx) * out_cols : (4 + dx) * out_cols] = low
            result = dot_t(woven[...], taps)
            for half in range(cols // 128):
                for k in range(planes * rows):
                    piece = result[k * channels : (k + 1) * channels, half * 128 : (half + 1) * 128]
                    lanes[pl.ds(k, channels, stride=planes * rows), :] = piece
                out_refs[h][:, half * 128 : (half + 1) * 128] = lanes[...]

    return pl.pallas_call(
        kernel,
        out_shape=[jax.ShapeDtypeStruct((channels * planes * rows, cols), F32)] * cores
        + [jax.ShapeDtypeStruct((chips * 128, 128 * chips), BF16)],
        scratch_shapes=[
            pltpu.VMEM((padded, 2 * count), F32),
            pltpu.VMEM((27 * ninth, 2 * count), BF16),
            pltpu.VMEM((8 * count, cells), BF16),
            pltpu.VMEM((third, cells), F32),
            pltpu.VMEM((third, cells), F32),
            pltpu.VMEM((planes * rows * channels, 6 * out_cols), BF16),
            pltpu.VMEM((planes * rows * channels, 128), F32),
        ],
        cost_estimate=pl.CostEstimate(flops=COVER, bytes_accessed=8000000, transcendentals=0),
        compiler_params=PARAMS,
        name="input_partial",
    )(*weights, *own, *[g.reshape(-1, out_cols) for g in grads])


def below(value, bits):
    parts, groups = lax.axis_size("gz"), lax.axis_size("af")
    pairs = [
        ((slab + 1) * groups + (a ^ bits), slab * groups + a) for slab in range(parts - 1) for a in range(groups)
    ]
    return lax.ppermute(value, ("gz", "af"), pairs)


def fast(volume, out_grad, weight):
    channels, planes, rows, cols = volume.shape
    filters, out_depth, out_rows, out_cols = out_grad.shape
    parts, cores = lax.axis_size("gz"), 2
    out_routes = [routes(parts, [place ^ (place >> 1) for place in range(parts)], k) for k in range(1, parts)]
    back_routes = [routes(parts, range(parts), k) for k in range(1, parts)]
    factor = 1.0 / math.sqrt(out_depth * parts * out_rows * out_cols)
    across = swapped(out_grad, "af", cores)
    above = [below(out_grad, 0), below(out_grad, cores)]
    high, low, *own, mine, theirs = prepare([volume, swapped(volume, "af", 1)], out_grad, weight)
    weights = [mine, swapped(theirs, "af", cores)]
    terms = weight_terms(high, low, own, across)
    sent = weight_partial(high, low, terms, above, out_routes)
    arrived = [sent[0]] + [routed(piece, "gz", route) for piece, route in zip(sent[1:], out_routes)]
    *inputs, place = input_partial(weights, own, [*above, across], volume.shape, cores)
    input_grad = (inputs[0] + swapped(inputs[1], "af", 1)).reshape(volume.shape)
    sums = add_slabs(arrived, 2, inputs[0])
    woven = weave_channels([sums[0], swapped(sums[1], "af", cores)], place, channels, cores, factor)
    pieces = [woven] + [routed(woven, "gz", route) for route in back_routes]
    input_grad, pieces = lax.optimization_barrier((input_grad, pieces))
    weight_grad = stack_slabs(pieces, back_routes)
    return (input_grad, weight_grad)


def tap_matrix(extended, out_depth, out_rows, out_cols):
    channels = extended.shape[0]
    padded = jnp.pad(extended, ((0, 0), (0, 1), (1, 1), (1, 1)))
    split = padded.reshape(channels, out_depth + 1, 2, out_rows + 1, 2, out_cols + 1, 2)
    pieces = []
    for depth_tap in range(3):
        for row_tap in range(3):
            for col_tap in range(3):
                dz_lo = depth_tap // 2
                dy_lo = row_tap // 2
                dx_lo = col_tap // 2
                pieces.append(
                    split[
                        :,
                        dz_lo : dz_lo + out_depth,
                        depth_tap % 2,
                        dy_lo : dy_lo + out_rows,
                        row_tap % 2,
                        dx_lo : dx_lo + out_cols,
                        col_tap % 2,
                    ]
                )
    stacked = jnp.stack(pieces, axis=0)
    return stacked.reshape(27 * channels, out_depth * out_rows * out_cols)


def place_terms(tap_terms, channels, depth_count, out_rows, out_cols, planes, rows, cols):
    shaped = tap_terms.reshape(27, channels, depth_count, out_rows, out_cols)
    phases = {}
    for depth_tap in range(3):
        for row_tap in range(3):
            for col_tap in range(3):
                index = 9 * depth_tap + 3 * row_tap + col_tap
                dz_lo = depth_tap // 2
                dy_lo = row_tap // 2
                dx_lo = col_tap // 2
                moved = jnp.pad(
                    shaped[index],
                    ((0, 0), (dz_lo, 1 - dz_lo), (dy_lo, 1 - dy_lo), (dx_lo, 1 - dx_lo)),
                )
                parity = (depth_tap % 2, row_tap % 2, col_tap % 2)
                phases[parity] = moved if parity not in phases else phases[parity] + moved
    depth_pairs = []
    for depth_bit in range(2):
        row_pairs = []
        for row_bit in range(2):
            col_pair = jnp.stack(
                [phases[depth_bit, row_bit, 0], phases[depth_bit, row_bit, 1]], axis=-1
            )
            row_pairs.append(col_pair)
        depth_pairs.append(jnp.stack(row_pairs, axis=3))
    woven = jnp.stack(depth_pairs, axis=2)
    canvas = woven.reshape(channels, 2 * (depth_count + 1), 2 * (out_rows + 1), 2 * (out_cols + 1))
    return canvas[:, 1 : planes + 1, 1 : rows + 1, 1 : cols + 1]


def general(volume, out_grad, weight):
    channels, planes, rows, cols = volume.shape
    filters, out_depth, out_rows, out_cols = out_grad.shape
    in_total = weight.shape[1] // 27
    factor = 1.0 / math.sqrt(out_depth * lax.axis_size("gz") * out_rows * out_cols)
    lower_rim = shifted(volume[:, planes - 1 : planes], "gz", 1)
    extended = jnp.concatenate([lower_rim, volume], axis=1)
    upper_rim = shifted(out_grad, "gz", -1)
    grad_ext = jnp.concatenate([out_grad, upper_rim], axis=1)
    grads_all, weight_all = (
        lax.all_gather(grad_ext, "af", axis=0, tiled=True),
        lax.all_gather(weight, "af", axis=0, tiled=True),
    )
    all_filters = grads_all.shape[0]
    channel_first = lax.axis_index("af") * channels
    weight_cube = weight_all.reshape(all_filters, 27, in_total)
    own_weight = lax.dynamic_slice_in_dim(weight_cube, channel_first, channels, 2).reshape(
        all_filters, 27 * channels
    )
    tap_terms = lax.dot_general(
        own_weight,
        grads_all.reshape(all_filters, -1),
        (((0,), (0,)), ((), ())),
        precision=lax.Precision.HIGHEST,
        preferred_element_type=jnp.float32,
    )
    input_grad = place_terms(
        tap_terms, channels, out_depth + 1, out_rows, out_cols, planes, rows, cols
    )
    local_grads = out_grad.reshape(filters, -1)
    portion = lax.all_gather(extended, "af", axis=0, tiled=True)
    count = portion.shape[0]
    tap_rows = tap_matrix(portion, out_depth, out_rows, out_cols)
    partial_grad = lax.dot_general(
        local_grads,
        tap_rows,
        (((1,), (1,)), ((), ())),
        precision=lax.Precision.HIGHEST,
        preferred_element_type=jnp.float32,
    )
    partial_grad = partial_grad.reshape(filters, 27, count)
    summed = lax.psum(partial_grad, "gz")
    weight_grad = (summed * factor).reshape(filters, 27 * in_total)
    return (input_grad, weight_grad)


def local(volume, out_grad, weight):
    channels, planes, rows, _ = volume.shape
    filters, out_depth, out_rows, _ = out_grad.shape
    parts, groups = lax.axis_size("gz"), lax.axis_size("af")
    powers = parts & (parts - 1) == 0 and groups == 4
    whole_tiles = channels == 16 and filters % (8 * parts) == 0 and filters == 32
    if powers and whole_tiles and (planes, out_depth) == (2, 1):
        return fast(volume, out_grad, weight)
    return general(volume, out_grad, weight)


def solution(mesh):
    return jax.shard_map(
        local,
        mesh=mesh,
        in_specs=(
            P("af", ("grp", "gz"), None, None),
            P("af", ("grp", "gz"), None, None),
            P("af", None),
        ),
        out_specs=(P("af", ("grp", "gz"), None, None), P("af", "grp")),
        check_vma=False,
    )
```

```python
import math

import jax
import jax.numpy as jnp
from jax import lax
from jax.experimental import pallas as pl
from jax.experimental.pallas import tpu as pltpu
from jax.sharding import PartitionSpec as P

F32 = jnp.float32
BF16 = jnp.bfloat16
VMEM = pl.BlockSpec(memory_space=pltpu.VMEM)
HBM = pl.BlockSpec(memory_space=pltpu.HBM)
COVER = 8000000000
PARAMS = pltpu.CompilerParams(vmem_limit_bytes=48 * 1024 * 1024)


def shifted(value, axis, steps):
    count = lax.axis_size(axis)
    leading, last = (max(0, -steps), min(count, count - steps))
    return lax.ppermute(value, axis, [(source, source + steps) for source in range(leading, last)])


def swapped(value, axis, bits):
    count = lax.axis_size(axis)
    return lax.ppermute(value, axis, [(source, source ^ bits) for source in range(count)])


def in_hbm(value):
    return pltpu.with_memory_space_constraint(value, pltpu.HBM)


def routes(count, ring, steps):
    place = {slab: at for at, slab in enumerate(ring)}
    return [ring[(place[slab] + steps) % count] for slab in range(count)]


def routed(value, axis, route):
    return lax.ppermute(value, axis, list(enumerate(route)))


def entry(table, index):
    value = table[0]
    for at in range(1, len(table)):
        value = jnp.where(index == at, table[at], value)
    return value


def halves(value):
    high = value.astype(BF16)
    return high, (value - high.astype(F32)).astype(BF16)


def dot(a, b):
    return lax.dot_general(a, b, (((1,), (0,)), ((), ())), preferred_element_type=F32)


def dot_t(a, b):
    return lax.dot_general(a, b, (((1,), (1,)), ((), ())), preferred_element_type=F32)


def column_taps(cols, out_cols):
    x = lax.broadcasted_iota(jnp.int32, (cols, 3 * out_cols), 0)
    c = lax.broadcasted_iota(jnp.int32, (cols, 3 * out_cols), 1)
    dx = c // out_cols
    return jnp.where(x == 2 * (c - dx * out_cols) + dx - 1, 1.0, 0.0).astype(BF16)


def split_rows(g_ref, filters, out_rows, out_cols, high_ref, low_ref, first=0):
    for q in range(out_rows):
        pair = halves(g_ref[pl.ds(q, filters, stride=out_rows), :])
        for target, half in zip((high_ref, low_ref), pair):
            target[first : first + filters, q * out_cols : (q + 1) * out_cols] = half


def pack_columns(w_ref, targets, total, kept, sides):
    filters, width = w_ref.shape
    span = 128 * total // kept
    row = lax.broadcasted_iota(jnp.int32, (span, 128), 0)
    col = lax.broadcasted_iota(jnp.int32, (span, 128), 1)
    start = (col // kept) * total + col % kept
    places = [jnp.where(row == start + side * kept, 1.0, 0.0).astype(BF16) for side in sides]
    for first in range(0, width, span):
        size = min(span, width - first)
        value = w_ref[:, first : first + size]
        if size < span:
            value = jnp.concatenate([value, jnp.zeros((filters, span - size), F32)], axis=1)
        high = value.astype(BF16).astype(F32)
        rest = value - high
        middle = rest.astype(BF16).astype(F32)
        stacked = jnp.concatenate([high, middle, rest - middle], axis=0).astype(BF16)
        at = first * kept // total
        for place, target in zip(places, targets):
            packed = dot(stacked, place)
            result = packed[:filters] + packed[filters : 2 * filters] + packed[2 * filters :]
            last = min(128, 27 * kept - at)
            target[:, at : at + last] = result[:, :last]


def prepare(volumes, out_grad, weight):
    filters, _, out_rows, out_cols = out_grad.shape
    channels, planes, rows, cols = volumes[0].shape
    cores = len(volumes)
    count = planes * rows * channels
    width = planes * 9 * cores * channels
    cells = out_rows * out_cols
    total, kept = weight.shape[1] // 27, cores * channels

    def kernel(v_hbm, g_hbm, w_hbm, *refs):
        v_refs = refs[: cores - 1]
        targets, g_targets = refs[cores - 1 : cores + 1], refs[cores + 1 : cores + 3]
        w_targets = refs[cores + 3 : cores + 5]
        x_refs, d_refs = refs[cores + 5 : cores + 7], refs[cores + 7 : cores + 9]
        own_lanes, lanes, g_ref, w_ref, sems = refs[cores + 9 :]
        copies = [
            pltpu.make_async_copy(v_hbm.at[:, h * 128 : (h + 1) * 128], own_lanes.at[h], sems.at[h])
            for h in range(cols // 128)
        ]
        copies.append(pltpu.make_async_copy(g_hbm, g_ref, sems.at[cols // 128]))
        copies.append(pltpu.make_async_copy(w_hbm, w_ref, sems.at[cols // 128 + 1]))
        for copy in copies:
            copy.start()
        taps = column_taps(cols, out_cols)
        for core in reversed(range(cores)):
            if core == 0:
                for copy in copies:
                    copy.wait()
            for h in range(cols // 128):
                source = own_lanes.at[h]
                if core:
                    source = lanes
                    lanes[...] = v_refs[core - 1][:, h * 128 : (h + 1) * 128]
                for k in range(planes * rows):
                    pair = halves(source[pl.ds(k, channels, stride=planes * rows), :])
                    for x_ref, half in zip(x_refs, pair):
                        x_ref[k * channels : (k + 1) * channels, h * 128 : (h + 1) * 128] = half
            for x_ref, d_ref, target in zip(x_refs, d_refs, targets):
                d_ref[...] = dot(x_ref[...], taps).astype(BF16)
                for z in range(planes):
                    for dy in range(3):
                        for q in range(out_rows):
                            y = 2 * q + dy - 1
                            for dx in range(3):
                                at = (((z * 3 + dy) * 3 + dx) * cores + core) * channels
                                if y < 0:
                                    piece = jnp.zeros((channels, out_cols), BF16)
                                else:
                                    first = (z * rows + y) * channels
                                    piece = d_ref[first : first + channels, dx * out_cols : (dx + 1) * out_cols]
                                target[at : at + channels, q * out_cols : (q + 1) * out_cols] = piece
        split_rows(g_ref, filters, out_rows, out_cols, *g_targets)
        chip = lax.axis_index("af") // cores
        pack_columns(w_ref, w_targets, total, kept, (chip, 1 - chip))

    return pl.pallas_call(
        kernel,
        in_specs=[HBM, HBM, HBM] + [VMEM] * (cores - 1),
        out_shape=[jax.ShapeDtypeStruct((width, cells), BF16)] * 2
        + [jax.ShapeDtypeStruct((filters, cells), BF16)] * 2
        + [jax.ShapeDtypeStruct((filters, 27 * kept), F32)] * 2,
        scratch_shapes=[pltpu.VMEM((count, cols), BF16)] * 2
        + [pltpu.VMEM((count, 3 * out_cols), BF16)] * 2
        + [
            pltpu.VMEM((cols // 128, count, 128), F32),
            pltpu.VMEM((count, 128), F32),
            pltpu.VMEM((filters * out_rows, out_cols), F32),
            pltpu.VMEM(weight.shape, F32),
            pltpu.SemaphoreType.DMA((cols // 128 + 2,)),
        ],
        compiler_params=PARAMS,
        name="prepare",
    )(in_hbm(volumes[0].reshape(-1, cols)), in_hbm(out_grad.reshape(-1, out_cols)), in_hbm(weight), *[v.reshape(-1, cols) for v in volumes[1:]])


def weight_terms(high, low, own, across):
    filters, _, out_rows, out_cols = across.shape
    cells = out_rows * out_cols

    def kernel(high_ref, low_ref, own_high, own_low, g_ref, out_ref, g_both):
        g_both[:filters, :] = own_high[...]
        g_both[2 * filters : 3 * filters, :] = own_low[...]
        split_rows(g_ref, filters, out_rows, out_cols, g_both.at[filters:], g_both.at[3 * filters :])
        both = dot_t(g_both[...], high_ref[...])
        out_ref[...] = both[: 2 * filters] + both[2 * filters :] + dot_t(g_both[: 2 * filters, :], low_ref[...])

    return pl.pallas_call(
        kernel,
        out_shape=jax.ShapeDtypeStruct((2 * filters, high.shape[0]), F32),
        scratch_shapes=[pltpu.VMEM((4 * filters, cells), BF16)],
        compiler_params=PARAMS,
        name="weight_terms",
    )(high, low, *own, across.reshape(-1, out_cols))


def weight_partial(high, low, terms, above, routes_out):
    parts = len(routes_out) + 1
    filters, _, out_rows, out_cols = above[0].shape
    cells = out_rows * out_cols
    third = high.shape[0] // 2
    block = filters // parts
    chips = len(above)
    count = chips * filters

    def kernel(high_ref, low_ref, terms_ref, *refs):
        g_refs, out_refs = refs[:chips], refs[chips : chips + parts]
        g_both, total = refs[chips + parts :]
        for j, g_ref in enumerate(g_refs):
            split_rows(g_ref, filters, out_rows, out_cols, g_both.at[:count], g_both.at[count:], j * filters)
        both = dot_t(g_both[...], high_ref[third:, :])
        total[:, :third] = both[:count] + both[count:] + dot_t(g_both[:count, :], low_ref[third:, :])
        total[:, third:] = terms_ref[...]
        slab = lax.axis_index("gz")
        for k in range(parts):
            target = slab if k == 0 else entry(routes_out[k - 1], slab)
            for j in range(chips):
                first = pl.multiple_of(j * filters + target * block, 8)
                out_refs[k][j * block : (j + 1) * block, :] = total[pl.ds(first, block), :]

    return pl.pallas_call(
        kernel,
        out_shape=[jax.ShapeDtypeStruct((chips * block, 3 * third), F32)] * parts,
        scratch_shapes=[
            pltpu.VMEM((2 * count, cells), BF16),
            pltpu.VMEM((count, 3 * third), F32),
        ],
        compiler_params=PARAMS,
        name="weight_partial",
    )(high, low, terms, *[g.reshape(-1, out_cols) for g in above])


def add_slabs(pieces, chips, after):
    rows, width = pieces[0].shape
    block = rows // chips

    def kernel(after_ref, *refs):
        for j in range(chips):
            value = refs[0][j * block : (j + 1) * block, :]
            for piece in refs[1 : len(pieces)]:
                value = value + piece[j * block : (j + 1) * block, :]
            refs[len(pieces) + j][...] = value

    return pl.pallas_call(
        kernel,
        in_specs=[pl.BlockSpec(memory_space=pl.ANY)] + [VMEM] * len(pieces),
        out_shape=[jax.ShapeDtypeStruct((block, width), F32)] * chips,
        compiler_params=PARAMS,
        name="add_slabs",
    )(after, *pieces)


def channel_places(me, chips, cores, channels):
    total = chips * cores * channels
    taps = 128 // (cores * channels)
    row = lax.broadcasted_iota(jnp.int32, (chips * 128, taps * total), 0)
    col = lax.broadcasted_iota(jnp.int32, (chips * 128, taps * total), 1)
    j = row // 128
    inner = row - j * 128
    tap = inner // (cores * channels)
    owner = me ^ (j * cores + (inner // channels) % cores)
    return jnp.where(col == tap * total + owner * channels + inner % channels, 1.0, 0.0).astype(BF16)


def weave_channels(pieces, place, channels, cores, factor):
    chips = len(pieces)
    block, width = pieces[0].shape
    total = chips * cores * channels
    span = 128
    taps = span // (cores * channels)
    chunks = -(-width // span)

    def kernel(place_ref, *refs):
        place = place_ref[...]
        for c in range(chunks):
            size = min(span, width - c * span)
            columns = []
            for j in range(chips):
                value = refs[j][:, c * span : c * span + size] * factor
                if size < span:
                    value = jnp.concatenate([value, jnp.zeros((block, span - size), F32)], axis=1)
                columns.append(value)
            wide = jnp.concatenate(columns, axis=1)
            high = wide.astype(BF16).astype(F32)
            rest = wide - high
            middle = rest.astype(BF16).astype(F32)
            stacked = jnp.concatenate([high, middle, rest - middle], axis=0).astype(BF16)
            woven = dot(stacked, place)
            result = woven[:block] + woven[block : 2 * block] + woven[2 * block :]
            first = c * taps * total
            last = min(first + taps * total, 27 * total)
            refs[chips][:, first:last] = result[:, : last - first]

    return pl.pallas_call(
        kernel,
        out_shape=jax.ShapeDtypeStruct((block, 27 * total), F32),
        cost_estimate=pl.CostEstimate(flops=COVER, bytes_accessed=8000000, transcendentals=0),
        compiler_params=PARAMS,
        name="weave_channels",
    )(place, *pieces)


def stack_slabs(pieces, back_routes):
    block, width = pieces[0].shape
    parts = len(pieces)
    anywhere = pl.BlockSpec(memory_space=pl.ANY)

    def kernel(*refs):
        slab = lax.axis_index("gz")
        copies = []
        for k in range(parts):
            source = slab if k == 0 else entry([back_routes[k - 1].index(at) for at in range(parts)], slab)
            copies.append(pltpu.make_async_copy(refs[k], refs[parts].at[source], refs[parts + 1].at[k]))
            copies[-1].start()
        for copy in copies:
            copy.wait()

    return pl.pallas_call(
        kernel,
        in_specs=[anywhere] * parts,
        out_specs=anywhere,
        out_shape=jax.ShapeDtypeStruct((parts, block, width), F32),
        scratch_shapes=[pltpu.SemaphoreType.DMA((parts,))],
        compiler_params=PARAMS,
        name="stack_slabs",
    )(*pieces).reshape(parts * block, width)


def input_partial(weights, own, grads, volume_shape, cores):
    channels, planes, rows, cols = volume_shape
    chips = len(weights)
    filters, _, out_rows, out_cols = grads[0].shape
    count = chips * filters
    cells = out_rows * out_cols
    ninth = cores * channels
    padded = -(-27 * ninth // 128) * 128
    third = 9 * ninth

    def kernel(*refs):
        w_refs, own_refs, g_refs = refs[:chips], refs[chips : chips + 2], refs[chips + 2 : 3 * chips + 1]
        out_refs, place_ref = refs[3 * chips + 1 : 3 * chips + 1 + cores], refs[3 * chips + 1 + cores]
        turned, a_both, g_all, t_even, t_odd, woven, lanes = refs[3 * chips + 2 + cores :]
        me = lax.axis_index("af")
        place_ref[...] = channel_places(me, chips, cores, channels)
        for first in range(0, padded, 128):
            size = min(128, 27 * ninth - first)
            value = jnp.concatenate([w[:, first : first + size] for w in w_refs], axis=0)
            high = value.astype(BF16).astype(F32)
            value = jnp.concatenate([high, value - high], axis=0)
            if size < 128:
                value = jnp.concatenate([value, jnp.zeros((2 * count, 128 - size), F32)], axis=1)
            turned[first : first + 128, :] = value.T
        core = me % cores
        for tap in range(27):
            for h in range(cores):
                first = pl.multiple_of(tap * ninth + (core ^ h) * channels, 8)
                at = (tap * cores + h) * channels
                a_both[at : at + channels, :] = turned[pl.ds(first, channels), :].astype(BF16)
        for half in range(2):
            g_all[2 * half * count : 2 * half * count + filters, :] = own_refs[half][...]
        for k, g_ref in enumerate(g_refs):
            side, j = (1, k) if k < chips else (0, k - chips + 1)
            first = side * 4 * count
            split_rows(g_ref, filters, out_rows, out_cols, g_all.at[first:], g_all.at[first + 2 * count :], j * filters)
        for at in range(0, 8 * count, 2 * count):
            g_all[at + count : at + 2 * count, :] = g_all[at : at + count, :]
        even = a_both[third : 2 * third, :]
        t_even[...] = dot(jnp.concatenate([even, even], axis=1), g_all[: 4 * count, :])
        odd, above = a_both[2 * third :, :], a_both[:third, :]
        t_odd[...] = dot(jnp.concatenate([odd, odd, above, above], axis=1), g_all[...])
        taps = column_taps(cols, out_cols)
        taps = jnp.concatenate([taps, taps], axis=1)
        for h in reversed(range(cores)):
            for z, terms in enumerate((t_even, t_odd)):
                for y in range(rows):
                    q = y // 2
                    for dx in range(3):

                        def term(dy, at):
                            first = (dy * 3 + dx) * ninth + h * channels
                            return terms[first : first + channels, at * out_cols : (at + 1) * out_cols]

                        if y % 2 == 0:
                            value = term(1, q)
                        else:
                            value = term(2, q)
                            if q + 1 < out_rows:
                                value = value + term(0, q + 1)
                        high, low = halves(value)
                        first = (z * rows + y) * channels
                        woven[first : first + channels, dx * out_cols : (dx + 1) * out_cols] = high
                        woven[first : first + channels, (3 + dx) * out_cols : (4 + dx) * out_cols] = low
            result = dot_t(woven[...], taps)
            for half in range(cols // 128):
                for k in range(planes * rows):
                    piece = result[k * channels : (k + 1) * channels, half * 128 : (half + 1) * 128]
                    lanes[pl.ds(k, channels, stride=planes * rows), :] = piece
                out_refs[h][:, half * 128 : (half + 1) * 128] = lanes[...]

    return pl.pallas_call(
        kernel,
        out_shape=[jax.ShapeDtypeStruct((channels * planes * rows, cols), F32)] * cores
        + [jax.ShapeDtypeStruct((chips * 128, 128 * chips), BF16)],
        scratch_shapes=[
            pltpu.VMEM((padded, 2 * count), F32),
            pltpu.VMEM((27 * ninth, 2 * count), BF16),
            pltpu.VMEM((8 * count, cells), BF16),
            pltpu.VMEM((third, cells), F32),
            pltpu.VMEM((third, cells), F32),
            pltpu.VMEM((planes * rows * channels, 6 * out_cols), BF16),
            pltpu.VMEM((planes * rows * channels, 128), F32),
        ],
        cost_estimate=pl.CostEstimate(flops=COVER, bytes_accessed=8000000, transcendentals=0),
        compiler_params=PARAMS,
        name="input_partial",
    )(*weights, *own, *[g.reshape(-1, out_cols) for g in grads])


def below(value, bits):
    parts, groups = lax.axis_size("gz"), lax.axis_size("af")
    pairs = [
        ((slab + 1) * groups + (a ^ bits), slab * groups + a) for slab in range(parts - 1) for a in range(groups)
    ]
    return lax.ppermute(value, ("gz", "af"), pairs)


def fast(volume, out_grad, weight):
    channels, planes, rows, cols = volume.shape
    filters, out_depth, out_rows, out_cols = out_grad.shape
    parts, cores = lax.axis_size("gz"), 2
    out_routes = [routes(parts, [place ^ (place >> 1) for place in range(parts)], k) for k in range(1, parts)]
    back_routes = [routes(parts, range(parts), k) for k in range(1, parts)]
    factor = 1.0 / math.sqrt(out_depth * parts * out_rows * out_cols)
    across = swapped(out_grad, "af", cores)
    above = [below(out_grad, 0), below(out_grad, cores)]
    high, low, *own, mine, theirs = prepare([volume, swapped(volume, "af", 1)], out_grad, weight)
    weights = [mine, swapped(theirs, "af", cores)]
    terms = weight_terms(high, low, own, across)
    sent = weight_partial(high, low, terms, above, out_routes)
    arrived = [sent[0]] + [routed(piece, "gz", route) for piece, route in zip(sent[1:], out_routes)]
    *inputs, place = input_partial(weights, own, [*above, across], volume.shape, cores)
    input_grad = (inputs[0] + swapped(inputs[1], "af", 1)).reshape(volume.shape)
    sums = add_slabs(arrived, 2, inputs[0])
    woven = weave_channels([sums[0], swapped(sums[1], "af", cores)], place, channels, cores, factor)
    pieces = [woven] + [routed(woven, "gz", route) for route in back_routes]
    input_grad, pieces = lax.optimization_barrier((input_grad, pieces))
    weight_grad = stack_slabs(pieces, back_routes)
    return (input_grad, weight_grad)


def tap_matrix(extended, out_depth, out_rows, out_cols):
    channels = extended.shape[0]
    padded = jnp.pad(extended, ((0, 0), (0, 1), (1, 1), (1, 1)))
    split = padded.reshape(channels, out_depth + 1, 2, out_rows + 1, 2, out_cols + 1, 2)
    pieces = []
    for depth_tap in range(3):
        for row_tap in range(3):
            for col_tap in range(3):
                dz_lo = depth_tap // 2
                dy_lo = row_tap // 2
                dx_lo = col_tap // 2
                pieces.append(
                    split[
                        :,
                        dz_lo : dz_lo + out_depth,
                        depth_tap % 2,
                        dy_lo : dy_lo + out_rows,
                        row_tap % 2,
                        dx_lo : dx_lo + out_cols,
                        col_tap % 2,
                    ]
                )
    stacked = jnp.stack(pieces, axis=0)
    return stacked.reshape(27 * channels, out_depth * out_rows * out_cols)


def place_terms(tap_terms, channels, depth_count, out_rows, out_cols, planes, rows, cols):
    shaped = tap_terms.reshape(27, channels, depth_count, out_rows, out_cols)
    phases = {}
    for depth_tap in range(3):
        for row_tap in range(3):
            for col_tap in range(3):
                index = 9 * depth_tap + 3 * row_tap + col_tap
                dz_lo = depth_tap // 2
                dy_lo = row_tap // 2
                dx_lo = col_tap // 2
                moved = jnp.pad(
                    shaped[index],
                    ((0, 0), (dz_lo, 1 - dz_lo), (dy_lo, 1 - dy_lo), (dx_lo, 1 - dx_lo)),
                )
                parity = (depth_tap % 2, row_tap % 2, col_tap % 2)
                phases[parity] = moved if parity not in phases else phases[parity] + moved
    depth_pairs = []
    for depth_bit in range(2):
        row_pairs = []
        for row_bit in range(2):
            col_pair = jnp.stack(
                [phases[depth_bit, row_bit, 0], phases[depth_bit, row_bit, 1]], axis=-1
            )
            row_pairs.append(col_pair)
        depth_pairs.append(jnp.stack(row_pairs, axis=3))
    woven = jnp.stack(depth_pairs, axis=2)
    canvas = woven.reshape(channels, 2 * (depth_count + 1), 2 * (out_rows + 1), 2 * (out_cols + 1))
    return canvas[:, 1 : planes + 1, 1 : rows + 1, 1 : cols + 1]


def general(volume, out_grad, weight):
    channels, planes, rows, cols = volume.shape
    filters, out_depth, out_rows, out_cols = out_grad.shape
    in_total = weight.shape[1] // 27
    factor = 1.0 / math.sqrt(out_depth * lax.axis_size("gz") * out_rows * out_cols)
    lower_rim = shifted(volume[:, planes - 1 : planes], "gz", 1)
    extended = jnp.concatenate([lower_rim, volume], axis=1)
    upper_rim = shifted(out_grad, "gz", -1)
    grad_ext = jnp.concatenate([out_grad, upper_rim], axis=1)
    grads_all, weight_all = (
        lax.all_gather(grad_ext, "af", axis=0, tiled=True),
        lax.all_gather(weight, "af", axis=0, tiled=True),
    )
    all_filters = grads_all.shape[0]
    channel_first = lax.axis_index("af") * channels
    weight_cube = weight_all.reshape(all_filters, 27, in_total)
    own_weight = lax.dynamic_slice_in_dim(weight_cube, channel_first, channels, 2).reshape(
        all_filters, 27 * channels
    )
    tap_terms = lax.dot_general(
        own_weight,
        grads_all.reshape(all_filters, -1),
        (((0,), (0,)), ((), ())),
        precision=lax.Precision.HIGHEST,
        preferred_element_type=jnp.float32,
    )
    input_grad = place_terms(
        tap_terms, channels, out_depth + 1, out_rows, out_cols, planes, rows, cols
    )
    local_grads = out_grad.reshape(filters, -1)
    portion = lax.all_gather(extended, "af", axis=0, tiled=True)
    count = portion.shape[0]
    tap_rows = tap_matrix(portion, out_depth, out_rows, out_cols)
    partial_grad = lax.dot_general(
        local_grads,
        tap_rows,
        (((1,), (1,)), ((), ())),
        precision=lax.Precision.HIGHEST,
        preferred_element_type=jnp.float32,
    )
    partial_grad = partial_grad.reshape(filters, 27, count)
    summed = lax.psum(partial_grad, "gz")
    weight_grad = (summed * factor).reshape(filters, 27 * in_total)
    return (input_grad, weight_grad)


def local(volume, out_grad, weight):
    channels, planes, rows, _ = volume.shape
    filters, out_depth, out_rows, _ = out_grad.shape
    parts, groups = lax.axis_size("gz"), lax.axis_size("af")
    powers = parts & (parts - 1) == 0 and groups == 4
    whole_tiles = channels == 16 and filters % (8 * parts) == 0 and filters == 32
    if powers and whole_tiles and (planes, out_depth) == (2, 1):
        return fast(volume, out_grad, weight)
    return general(volume, out_grad, weight)


def solution(mesh):
    return jax.shard_map(
        local,
        mesh=mesh,
        in_specs=(
            P("af", ("grp", "gz"), None, None),
            P("af", ("grp", "gz"), None, None),
            P("af", None),
        ),
        out_specs=(P("af", ("grp", "gz"), None, None), P("af", "grp")),
        check_vma=False,
    )
```
